32 devices in a mesh: narrow: 2 (over y), wide: 16 (over z, x, core).
Axes of the slice: x: 2, y: 2, z: 4, core: 2. Of those that a mesh axis runs over, the one named last changes fastest.
Arguments:
- layer_input: bfloat16 [2, 2048, 2048], P('narrow', 'wide'), may hold values from -6 to 6
- lengths: int32 [2], P('narrow'), may hold values from 768 to 2048, as said below
- attn_gain: bfloat16 [2048], replicated, may hold values from 0.5 to 1.5
- w_query: bfloat16 [2048, 2048], P('wide'), may hold values from -0.125 to 0.125
- w_key: bfloat16 [2048, 2048], P('wide'), may hold values from -0.125 to 0.125
- w_value: bfloat16 [2048, 2048], P('wide'), may hold values from -0.125 to 0.125
- w_out: bfloat16 [2048, 2048], P('wide'), may hold values from -3 to 3
- mlp_gain: bfloat16 [2048], replicated, may hold values from 0.5 to 1.5
- w_gate: bfloat16 [8192, 2048], P('wide'), may hold values from -0.125 to 0.125
- w_up: bfloat16 [8192, 2048], P('wide'), may hold values from -0.125 to 0.125
- w_down: bfloat16 [8192, 2048], P('wide'), may hold values from -0.0625 to 0.0625
- cotangent: bfloat16 [2, 2048, 2048], P('narrow', 'wide'), may hold values from -8 to 8
Outputs:
- block_output: bfloat16 [2, 2048, 2048], P('narrow', 'wide')
- input_grad: float32 [2, 2048, 2048], P('narrow', 'wide')
- grad_attn_gain: float32 [2048], replicated
- grad_query: float32 [2048, 2048], P('wide')
- grad_key: float32 [2048, 2048], P('wide')
- grad_value: float32 [2048, 2048], P('wide')
- grad_out: float32 [2048, 2048], P('wide')
- grad_mlp_gain: float32 [2048], replicated
- grad_gate: float32 [8192, 2048], P('wide')
- grad_up: float32 [8192, 2048], P('wide')
- grad_down: float32 [8192, 2048], P('wide')
The draws below stay inside these ranges and needn't reach their ends.
Inputs may be any that keep to these rules, and one draw needn't show every extreme that they name: `lengths`: valid positions of each sequence, counted from its start; in every draw one sequence fills all 2048 positions.
All inputs are finite; a program needn't handle non-finite values.
Results may differ from the reference program's by a relative error of at most 0.017.
Values may be sent and summed in bfloat16 or wider, within the bound.
No kernel may reach another device: no remote copies, remote signals or barrier semaphores. Data moves between devices by JAX's collectives and lax.ppermute only.
A program may use at most 768 MiB of HBM per device.

```python
import math
import jax
import jax.numpy as jnp
from jax import lax

D = 2048
HEADS = 32
HEAD_DIM = 64
FF = 8192
SEQ_LEN = 2048
SEQS = 2


def draw_lengths(key, part):
    pick_key, fill_key = jax.random.split(jax.random.fold_in(key, 17))
    sampled = jax.random.randint(pick_key, (SEQS,), 3 * SEQ_LEN // 8, SEQ_LEN + 1)
    chosen = jax.random.randint(fill_key, (), 0, SEQS)
    return jnp.where(jnp.arange(SEQS) == chosen, SEQ_LEN, sampled).astype(jnp.int32)


def with_spikes(values, rng, source, target, shards_of, factor):
    owner, partner = [(jnp.arange(values.shape[dim]) // (values.shape[dim] // shards_of)).reshape([-1 if axis == dim else 1 for axis in range(values.ndim)]) for dim in (source, target)]
    chosen = jax.random.permutation(rng, shards_of)[partner]
    strong = (owner == chosen) | (owner == (partner + shards_of // 2) % shards_of)
    return jnp.where(strong, factor * values, values)


def block_scale(rng, dims, cuts, low, largest):
    def one(dim, shards_of):
        heights = jax.random.uniform(jax.random.fold_in(jax.random.fold_in(rng, 6), dim), (shards_of,), jnp.float32, low / len(cuts), largest / len(cuts))
        return jnp.repeat(jnp.exp(heights), dims[dim] // shards_of).reshape((-1,) + (1,) * (len(dims) - dim - 1))

    loudness = one(*cuts[0])
    for cut in cuts[1:]:
        loudness = loudness * one(*cut)
    return loudness


def scatter_about(stream_key, dims, spread, reach, pieces=(), held_as=jnp.bfloat16):
    result = spread * jax.random.normal(stream_key, dims, jnp.float32)
    if pieces:
        result = result * block_scale(stream_key, dims, pieces, -0.22, 0.18)
    return jnp.clip(result, -reach, reach).astype(held_as)


def noise_with(stream_key, dims, spread, bound, pieces, heavy, held_as=jnp.bfloat16):
    array = spread * jax.random.normal(stream_key, dims, jnp.float32)
    if pieces:
        array = array * block_scale(stream_key, dims, pieces, -0.22, 0.18)
    return jnp.clip(with_spikes(array, jax.random.fold_in(stream_key, 3), *heavy), -bound, bound).astype(held_as)


def setup_inputs(seed: int = 0) -> dict:
    streams_of = jax.random.split(jax.random.key(seed), 13)
    return {
        "layer_input": noise_with(streams_of[0], (SEQS, SEQ_LEN, D), 1.0, 6.0, ((0, 2), (1, 16)), (1, 2, 16, 2.0)),
        "lengths": draw_lengths(jax.random.fold_in(streams_of[12], 71), 0),
        "attn_gain": jnp.clip(1.0 + 0.1 * jax.random.normal(streams_of[2], (D,), jnp.float32), 0.5, 1.5).astype(jnp.bfloat16),
        "w_query": scatter_about(streams_of[3], (D, D), D ** -0.5, 0.125, ((0, 16),)),
        "w_key": scatter_about(streams_of[4], (D, D), D ** -0.5, 0.125, ((0, 16),)),
        "w_value": scatter_about(streams_of[5], (D, D), D ** -0.5, 0.125, ((0, 16),)),
        "w_out": scatter_about(streams_of[6], (D, D), (max(1, 4 * D // SEQ_LEN)) ** -0.5, 3.0, ((0, 16),)),
        "mlp_gain": jnp.clip(1.0 + 0.1 * jax.random.normal(streams_of[7], (D,), jnp.float32), 0.5, 1.5).astype(jnp.bfloat16),
        "w_gate": scatter_about(streams_of[8], (FF, D), D ** -0.5, 0.125, ((0, 16),)),
        "w_up": scatter_about(streams_of[9], (FF, D), D ** -0.5, 0.125, ((0, 16),)),
        "w_down": scatter_about(streams_of[10], (FF, D), FF ** -0.5, 0.0625, ((0, 16),)),
        "cotangent": scatter_about(streams_of[11], (SEQS, SEQ_LEN, D), 2.0, 8.0, ((0, 2), (1, 16))),
    }


EPSILON = 1e-05
THETA = 130000.0
NEGATIVE = -1e+30
HIGHEST = lax.Precision.HIGHEST

@jax.custom_vjp
def low(v):
    return lax.optimization_barrier(v.astype(jnp.bfloat16)).astype(jnp.float32)

@jax.custom_vjp
def low_back(v):
    return v

def low_keep(v):
    return (low(v), None)

def low_pass(kept, grad):
    return (grad,)

def back_keep(v):
    return (v, None)

def back_low(kept, grad):
    return (low(grad),)
low.defvjp(low_keep, low_pass)
low_back.defvjp(back_keep, back_low)

def matmul(left_side, right_side):
    return jnp.dot(left_side, right_side, precision=HIGHEST)

def matmul_cols(left_side, right_side):
    return jnp.dot(left_side, right_side.T, precision=HIGHEST)

def rms_norm(matrix, gain_vec):
    return matrix * lax.rsqrt(lax.optimization_barrier(jnp.mean(matrix * matrix, axis=-1, keepdims=True)) + EPSILON) * gain_vec

def rotate(tensor):
    half_dim = tensor.shape[-1] // 2
    return jnp.concatenate([-tensor[..., half_dim:], tensor[..., :half_dim]], axis=-1)

def rotary(tensor):
    half_dim = HEAD_DIM // 2
    frequency = THETA ** (-jnp.arange(half_dim, dtype=jnp.float32) * 2.0 / HEAD_DIM)
    angles = jnp.arange(SEQ_LEN, dtype=jnp.float32)[:, None] * frequency[None, :]
    cosine_table = jnp.concatenate([jnp.cos(angles), jnp.cos(angles)], axis=-1)[:, None, :]
    sine_table = jnp.concatenate([jnp.sin(angles), jnp.sin(angles)], axis=-1)[:, None, :]
    return tensor * cosine_table + rotate(tensor) * sine_table

def attend(query, key_rot, value_heads, length):
    block_size = math.gcd(SEQ_LEN, 512)
    block_count = SEQ_LEN // block_size
    score_scale = HEAD_DIM ** (-0.5)
    key_pos = jnp.arange(SEQ_LEN, dtype=jnp.int32)

    def attend_block(scan_item):
        query_block, block_index = scan_item
        query_pos = block_index * block_size + jnp.arange(block_size, dtype=jnp.int32)
        raw_scores = jnp.einsum('qhd,khd->hqk', query_block, key_rot, precision=HIGHEST)
        scores = low_back(raw_scores) * score_scale
        allowed = ((key_pos[None, :] <= query_pos[:, None]) & (key_pos[None, :] < length))[None]
        scores = jnp.where(allowed, scores, NEGATIVE)
        row_top = lax.optimization_barrier(jnp.max(scores, axis=-1, keepdims=True))
        log_total = row_top + jnp.log(lax.optimization_barrier(jnp.sum(jnp.exp(scores - row_top), axis=-1, keepdims=True)))
        probs = jnp.where(allowed, jnp.exp(scores - log_total), 0.0)
        return jnp.einsum('hqk,khd->qhd', low(probs), value_heads, precision=HIGHEST)
    blocks = query.reshape(block_count, block_size, HEADS, HEAD_DIM)
    results = lax.map(jax.checkpoint(attend_block), (blocks, jnp.arange(block_count, dtype=jnp.int32)))
    return results.reshape(SEQ_LEN, HEADS * HEAD_DIM)

def decoder_layer(inputs, gain_one, w_query, w_key, w_value, w_out, gain_two, w_gate, w_up, w_down, length):
    norm_one = low(rms_norm(inputs, gain_one))
    query = low(rotary(low_back(matmul(norm_one, w_query)).reshape(SEQ_LEN, HEADS, HEAD_DIM)))
    key_rot = low(rotary(low_back(matmul(norm_one, w_key)).reshape(SEQ_LEN, HEADS, HEAD_DIM)))
    value_heads = low(low_back(matmul(norm_one, w_value))).reshape(SEQ_LEN, HEADS, HEAD_DIM)
    attention = low(low_back(attend(query, key_rot, value_heads, length)))
    residual = inputs + low_back(matmul(attention, w_out))
    norm_two = low(rms_norm(residual, gain_two))
    gate_proj = low_back(matmul_cols(norm_two, w_gate))
    up_proj = low_back(matmul_cols(norm_two, w_up))
    hidden = low(jax.nn.silu(gate_proj) * up_proj)
    return residual + low_back(matmul(hidden, w_down))

def reference(layer_input, lengths, attn_gain, w_query, w_key, w_value, w_out, mlp_gain, w_gate, w_up, w_down, cotangent):
    weight_args = tuple((member.astype(jnp.float32) for member in (attn_gain, w_query, w_key, w_value, w_out, mlp_gain, w_gate, w_up, w_down)))
    inputs = layer_input.astype(jnp.float32)
    cot_float = cotangent.astype(jnp.float32)
    positions = jnp.arange(SEQ_LEN, dtype=jnp.int32)

    def one_sequence(totals_carry, scan_item):
        seq_input, seq_back, length = scan_item

        def forward(seq_values, *weights):
            return decoder_layer(seq_values, *weights, length)
        output, pullback = jax.vjp(forward, seq_input, *weight_args)
        valid_rows = (positions < length).astype(jnp.float32)[:, None]
        gradients = pullback(seq_back * valid_rows)
        totals_carry = tuple((running + gradient for running, gradient in zip(totals_carry, gradients[1:])))
        return (totals_carry, (output.astype(jnp.bfloat16), gradients[0]))
    zero_grads = tuple((jnp.zeros_like(member) for member in weight_args))
    totals, results = lax.scan(one_sequence, zero_grads, (inputs, cot_float, lengths))
    return (results[0], results[1], totals[0], totals[1], totals[2], totals[3], totals[4], totals[5], totals[6], totals[7], totals[8])
```

```python
import functools
import jax
import jax.numpy as jnp
from jax import lax
from jax.experimental import pallas as pl
from jax.experimental.pallas import tpu as pltpu
import numpy as np
from jax.sharding import PartitionSpec as P

HEAD_DIM = 64
NEGATIVE = -1e30
VMEM_LIMIT = 56 * 1024 * 1024


def dot_nt(a, b):
    return lax.dot_general(a, b, (((1,), (1,)), ((), ())), preferred_element_type=jnp.float32)


def dot_nn(a, b):
    return lax.dot_general(a, b, (((1,), (0,)), ((), ())), preferred_element_type=jnp.float32)


def half_turn(tensor):
    width = tensor.shape[-1]
    half_dim = HEAD_DIM // 2
    lane = lax.broadcasted_iota(jnp.int32, tensor.shape, 1)
    return jnp.where(
        lane % HEAD_DIM < half_dim,
        -pltpu.roll(tensor, width - half_dim, 1),
        pltpu.roll(tensor, half_dim, 1),
    )


def head_lanes(block, head):
    lane = lax.broadcasted_iota(jnp.int32, block.shape, 1)
    return jnp.where(lane // HEAD_DIM == head, block, jnp.zeros_like(block))


def forward_kernel(
    slot_ref, length_ref, lin_ref, cos_ref, sin_ref,
    att_ref, query_ref, key_ref, value_ref, log_ref,
    turned, attn_nat,
):
    rows = query_ref.shape[0]
    width = query_ref.shape[1]
    heads = width // HEAD_DIM
    slots = slot_ref.shape[0]
    shard = rows // slots
    length = length_ref[0]
    scale = HEAD_DIM ** (-0.5)

    @pl.loop(0, slots)
    def _(place):
        source = pl.ds(pl.multiple_of(slot_ref[place] * shard, shard), shard)
        target = pl.ds(pl.multiple_of(place * shard, shard), shard)
        cosine = cos_ref[target, :]
        sine = sin_ref[target, :]
        query_lin = lin_ref[source, 0:width]
        key_lin = lin_ref[source, width : 2 * width]
        value_lin = lin_ref[source, 2 * width : 3 * width]
        query = (query_lin * cosine + half_turn(query_lin) * sine).astype(jnp.bfloat16)
        query_ref[target, :] = (query.astype(jnp.float32) * scale).astype(jnp.bfloat16)
        key_ref[target, :] = (key_lin * cosine + half_turn(key_lin) * sine).astype(jnp.bfloat16)
        value_ref[target, :] = value_lin.astype(jnp.bfloat16)
        turned[:, target] = value_lin.T.astype(jnp.bfloat16)

    block_q = min(256, rows)
    block_k = min(512, rows)

    @pl.loop(0, rows // block_q)
    def _(i):
        q_first = pl.multiple_of(i * block_q, block_q)
        query = query_ref[pl.ds(q_first, block_q), :]
        parts = [head_lanes(query, h) for h in range(heads)]
        q_pos = q_first + lax.broadcasted_iota(jnp.int32, (1, block_q), 1)
        limit = jnp.minimum(q_pos, length - 1)
        full = jnp.minimum(q_first, length) // block_k
        stop = (jnp.minimum(q_first + block_q, length) + block_k - 1) // block_k

        def step(j, state, masked):
            k_first = pl.multiple_of(j * block_k, block_k)
            key = key_ref[pl.ds(k_first, block_k), :]
            out = []
            if masked:
                k_pos = k_first + lax.broadcasted_iota(jnp.int32, (block_k, block_q), 0)
                allowed = k_pos <= limit
            for h in range(heads):
                best, total, acc = state[3 * h : 3 * h + 3]
                scores = dot_nt(key, parts[h])
                if masked:
                    scores = jnp.where(allowed, scores, NEGATIVE)
                new_best = jnp.maximum(best, jnp.max(scores, axis=0, keepdims=True))
                weight = jnp.exp(scores - new_best)
                shrink = jnp.exp(best - new_best)
                total = total * shrink + jnp.sum(weight, axis=0, keepdims=True)
                value_t = turned[h * HEAD_DIM : (h + 1) * HEAD_DIM, pl.ds(k_first, block_k)]
                acc = acc * shrink + dot_nn(value_t, weight.astype(jnp.bfloat16))
                out += [new_best, total, acc]
            return tuple(out)

        state = ()
        for h in range(heads):
            state += (
                jnp.full((1, block_q), NEGATIVE, jnp.float32),
                jnp.zeros((1, block_q), jnp.float32),
                jnp.zeros((HEAD_DIM, block_q), jnp.float32),
            )
        state = lax.fori_loop(0, full, functools.partial(step, masked=False), state)
        state = lax.fori_loop(full, stop, functools.partial(step, masked=True), state)
        for h in range(heads):
            best, total, acc = state[3 * h : 3 * h + 3]
            log_ref[h : h + 1, pl.ds(q_first, block_q)] = best + jnp.log(total)
        joined = jnp.concatenate([state[3 * h + 2] / state[3 * h + 1] for h in range(heads)], axis=0)
        attn_nat[pl.ds(q_first, block_q), :] = joined.T.astype(jnp.bfloat16)

    @pl.loop(0, slots)
    def _(place):
        source = pl.ds(pl.multiple_of(slot_ref[place] * shard, shard), shard)
        target = pl.ds(pl.multiple_of(place * shard, shard), shard)
        att_ref[source, :] = attn_nat[target, :]


def attention_forward(slot_of, length, lin, cosine, sine):
    rows, width = cosine.shape
    vmem = pl.BlockSpec(memory_space=pltpu.VMEM)
    smem = pl.BlockSpec(memory_space=pltpu.SMEM)
    half = jax.ShapeDtypeStruct((rows, width), jnp.bfloat16)
    return pl.pallas_call(
        forward_kernel,
        out_shape=(half, half, half, half, jax.ShapeDtypeStruct((8, rows), jnp.float32)),
        in_specs=[smem, smem, vmem, vmem, vmem],
        out_specs=(vmem,) * 5,
        scratch_shapes=[
            pltpu.VMEM((width, rows), jnp.bfloat16),
            pltpu.VMEM((rows, width), jnp.bfloat16),
        ],
        compiler_params=pltpu.CompilerParams(vmem_limit_bytes=VMEM_LIMIT),
        cost_estimate=pl.CostEstimate(
            flops=4 * rows * rows * width, bytes_accessed=24 * rows * width, transcendentals=rows * rows
        ),
        name="attention_forward",
    )(slot_of, length, lin, cosine, sine)


def backward_kernel(
    slot_ref, length_ref, query_ref, key_ref, value_ref, att_ref, up_ref, log_ref, cos_ref, sin_ref,
    out_ref,
    key_t, up_nat, delta, key_acc, value_acc, query_acc,
):
    rows = query_ref.shape[0]
    width = query_ref.shape[1]
    heads = width // HEAD_DIM
    slots = slot_ref.shape[0]
    shard = rows // slots
    length = length_ref[0]
    scale = HEAD_DIM ** (-0.5)
    key_acc[...] = jnp.zeros_like(key_acc)
    value_acc[...] = jnp.zeros_like(value_acc)

    @pl.loop(0, slots)
    def _(place):
        source = pl.ds(pl.multiple_of(slot_ref[place] * shard, shard), shard)
        target = pl.ds(pl.multiple_of(place * shard, shard), shard)
        upstream = up_ref[source, :]
        up_nat[target, :] = upstream
        product = (upstream.astype(jnp.float32) * att_ref[source, :].astype(jnp.float32)).T
        for h in range(heads):
            delta[h : h + 1, target] = jnp.sum(
                product[h * HEAD_DIM : (h + 1) * HEAD_DIM, :], axis=0, keepdims=True
            )
        key_t[:, target] = key_ref[target, :].astype(jnp.float32).T.astype(jnp.bfloat16)

    block_q = min(256, rows)
    block_k = min(512, rows)

    @pl.loop(0, rows // block_q)
    def _(i):
        q_first = pl.multiple_of(i * block_q, block_q)
        here = pl.ds(q_first, block_q)
        query = query_ref[here, :]
        upstream = up_nat[here, :]
        q_parts = [head_lanes(query, h) for h in range(heads)]
        u_parts = [head_lanes(upstream, h) for h in range(heads)]
        logs = [log_ref[h : h + 1, here] for h in range(heads)]
        deltas = [delta[h : h + 1, here] for h in range(heads)]
        q_pos = q_first + lax.broadcasted_iota(jnp.int32, (1, block_q), 1)
        limit = jnp.minimum(q_pos, length - 1)
        full = jnp.minimum(q_first, length) // block_k
        stop = (jnp.minimum(q_first + block_q, length) + block_k - 1) // block_k

        def step(j, state, masked):
            k_first = pl.multiple_of(j * block_k, block_k)
            there = pl.ds(k_first, block_k)
            key = key_ref[there, :]
            value = value_ref[there, :]
            if masked:
                k_pos = k_first + lax.broadcasted_iota(jnp.int32, (block_k, block_q), 0)
                allowed = k_pos <= limit
            out = []
            key_add = None
            for h in range(heads):
                prob = jnp.exp(dot_nt(key, q_parts[h]) - logs[h])
                if masked:
                    prob = jnp.where(allowed, prob, 0.0)
                pulled = dot_nt(value, u_parts[h])
                score_back = (prob * (pulled - deltas[h])).astype(jnp.bfloat16)
                one = dot_nn(prob.astype(jnp.bfloat16), u_parts[h])
                two = dot_nn(score_back, q_parts[h])
                value_add = one if key_add is None else value_add + one
                key_add = two if key_add is None else key_add + two
                out.append(
                    state[h] + dot_nn(key_t[h * HEAD_DIM : (h + 1) * HEAD_DIM, there], score_back)
                )
            value_acc[there, :] += value_add
            key_acc[there, :] += key_add
            return tuple(out)

        state = tuple(jnp.zeros((HEAD_DIM, block_q), jnp.float32) for h in range(heads))
        state = lax.fori_loop(0, full, functools.partial(step, masked=False), state)
        state = lax.fori_loop(full, stop, functools.partial(step, masked=True), state)
        query_acc[here, :] = (jnp.concatenate(state, axis=0) * scale).T

    @pl.loop(0, slots)
    def _(place):
        source = pl.ds(pl.multiple_of(slot_ref[place] * shard, shard), shard)
        target = pl.ds(pl.multiple_of(place * shard, shard), shard)
        cosine = cos_ref[target, :]
        sine = sin_ref[target, :]
        for piece, held in enumerate((query_acc, key_acc)):
            grad = held[target, :]
            out_ref[source, piece * width : (piece + 1) * width] = (
                grad * cosine - half_turn(grad * sine)
            ).astype(jnp.bfloat16)
        out_ref[source, 2 * width : 3 * width] = value_acc[target, :].astype(jnp.bfloat16)


def attention_backward(slot_of, length, query, key, value, att, upstream, logs, cosine, sine):
    rows, width = query.shape
    vmem = pl.BlockSpec(memory_space=pltpu.VMEM)
    smem = pl.BlockSpec(memory_space=pltpu.SMEM)
    return pl.pallas_call(
        backward_kernel,
        out_shape=jax.ShapeDtypeStruct((rows, 3 * width), jnp.bfloat16),
        in_specs=[smem, smem] + [vmem] * 8,
        out_specs=vmem,
        scratch_shapes=[
            pltpu.VMEM((width, rows), jnp.bfloat16),
            pltpu.VMEM((rows, width), jnp.bfloat16),
            pltpu.VMEM((8, rows), jnp.float32),
            pltpu.VMEM((rows, width), jnp.float32),
            pltpu.VMEM((rows, width), jnp.float32),
            pltpu.VMEM((rows, width), jnp.float32),
        ],
        compiler_params=pltpu.CompilerParams(vmem_limit_bytes=VMEM_LIMIT),
        cost_estimate=pl.CostEstimate(
            flops=10 * rows * rows * width, bytes_accessed=36 * rows * width, transcendentals=rows * rows
        ),
        name="attention_backward",
    )(slot_of, length, query, key, value, att, upstream, logs, cosine, sine)


EPSILON = 1e-05
THETA = 130000.0


def contract_rows(left_side, right_side):
    return lax.dot_general(
        left_side, right_side, (((0,), (0,)), ((), ())), preferred_element_type=jnp.float32
    )


def rotary_tables(row_count, width):
    half_dim = HEAD_DIM // 2
    frequency = THETA ** (-jnp.arange(half_dim, dtype=jnp.float32) * 2.0 / HEAD_DIM)
    angles = jnp.arange(row_count, dtype=jnp.float32)[:, None] * frequency[None, :]
    copies = width // half_dim
    return (jnp.tile(jnp.cos(angles), (1, copies)), jnp.tile(jnp.sin(angles), (1, copies)))


def rms_factor(matrix):
    return lax.rsqrt(jnp.mean(matrix * matrix, axis=-1, keepdims=True) + EPSILON)


def norm_back(upstream, normed, gain_vec, factor):
    scaled = upstream * gain_vec
    return factor * (scaled - normed * jnp.mean(scaled * normed, axis=-1, keepdims=True))


def swiglu_back(hidden_back, gate_proj, up_proj):
    sigmoid_gate = jax.nn.sigmoid(gate_proj)
    gate_back = hidden_back * up_proj * sigmoid_gate * (1.0 + gate_proj * (1.0 - sigmoid_gate))
    up_back = hidden_back * jax.nn.silu(gate_proj)
    return (gate_back.astype(jnp.bfloat16), up_back.astype(jnp.bfloat16))


class Ring:
    def __init__(self, size):
        self.size = size
        self.pairs = size // 2
        self.reach = self.pairs // 2
        columns = self.pairs // 2
        self.order = [2 * a for a in range(columns)] + [2 * a + 1 for a in reversed(range(columns))]
        self.ahead = []
        self.behind = []
        for place, pair in enumerate(self.order):
            following = self.order[(place + 1) % self.pairs]
            for lane in range(2):
                self.ahead.append((2 * pair + lane, 2 * following + lane))
                self.behind.append((2 * following + lane, 2 * pair + lane))
        self.across = [(device, device ^ 1) for device in range(size)]

    def slots(self):
        offsets = [(0, 0), (0, 1)]
        for step in range(1, self.reach):
            offsets += [(-step, 0), (step, 0), (-step, 1), (step, 1)]
        offsets += [(self.reach, 0), (self.reach, 1)]
        table = np.zeros((self.size, self.size), np.int32)
        for device in range(self.size):
            place = self.order.index(device // 2)
            for slot, (offset, flip) in enumerate(offsets):
                pair = self.order[(place + offset) % self.pairs]
                table[device, 2 * pair + (device % 2 ^ flip)] = slot
        return table

    def forward(self, array):
        return lax.ppermute(array, "wide", self.ahead)

    def backward(self, array):
        return lax.ppermute(array, "wide", self.behind)

    def twin(self, array):
        return lax.ppermute(array, "wide", self.across)

    def gather(self, rows):
        groups = [[rows, self.twin(rows)]]
        ahead = behind = rows
        middle = rows.shape[0] // 2
        for step in range(1, self.reach + 1):
            if step == self.reach:
                ahead, behind = ahead[:middle], behind[middle:]
            ahead, behind = self.forward(ahead), self.backward(behind)
            groups.append([ahead, behind, self.twin(ahead), self.twin(behind)])
        return [jnp.concatenate(group, axis=0) for group in groups]

    def scatter(self, make):
        sums = [None] * (self.reach + 1)
        down = up = None
        for step in range(self.reach, -1, -1):
            mine, other = make(step)
            total = mine + self.twin(other.astype(jnp.bfloat16)).astype(jnp.float32)
            count = total.shape[0] // 2
            if step == 0:
                return total + down.astype(jnp.float32) + up.astype(jnp.float32)
            low, high = total[:count], total[count:]
            if step == self.reach - 1:
                middle = count // 2
                low = jnp.concatenate([low[:middle] + down.astype(jnp.float32), low[middle:]], axis=0)
                high = jnp.concatenate([high[:middle], high[middle:] + up.astype(jnp.float32)], axis=0)
            elif step < self.reach - 1:
                low = low + down.astype(jnp.float32)
                high = high + up.astype(jnp.float32)
            down = self.backward(low.astype(jnp.bfloat16))
            up = self.forward(high.astype(jnp.bfloat16))

    def total(self, array):
        array = array + lax.ppermute(array, "narrow", [(0, 1), (1, 0)])
        bit = 1
        while bit < self.size:
            array = array + lax.ppermute(array, "wide", [(i, i ^ bit) for i in range(self.size)])
            bit *= 2
        return array


def both_sequences(part):
    part = lax.optimization_barrier(part.astype(jnp.bfloat16))
    return part.astype(jnp.float32) + lax.ppermute(part, "narrow", [(0, 1), (1, 0)]).astype(
        jnp.float32
    )


def halves(array):
    middle = array.shape[0] // 2
    return array[:middle], array[middle:]


def shards(
    ring,
    layer_input,
    lengths,
    attn_gain,
    w_query,
    w_key,
    w_value,
    w_out,
    mlp_gain,
    w_gate,
    w_up,
    w_down,
    cotangent,
):
    size = ring.size
    local_rows = layer_input.shape[1]
    model_width = layer_input.shape[2]
    row_count = local_rows * size
    own_width = model_width // size
    width = max(own_width, 2 * HEAD_DIM)
    sharing = width // own_width
    device = lax.axis_index("wide")
    member = device % sharing
    slot_of = lax.dynamic_index_in_dim(jnp.asarray(ring.slots()), device, keepdims=False)

    def own_columns(array):
        if sharing == 1:
            return array
        runs = array.reshape(array.shape[0], -1, sharing, own_width)
        return lax.dynamic_index_in_dim(runs, member, axis=2, keepdims=False).reshape(
            array.shape[0], -1
        )

    positions = device * local_rows + jnp.arange(local_rows, dtype=jnp.int32)
    valid_rows = (positions < lengths[0]).astype(jnp.float32)[:, None]
    cosine, sine = rotary_tables(row_count, width)
    inputs = layer_input[0].astype(jnp.float32)
    gain_one = attn_gain.astype(jnp.float32)
    gain_two = mlp_gain.astype(jnp.float32)
    y_back = cotangent[0].astype(jnp.float32) * valid_rows
    mlp_back = y_back.astype(jnp.bfloat16)

    blocks = jnp.concatenate(
        [w.reshape(own_width, -1, width) for w in (w_query, w_key, w_value)], axis=-1
    ).transpose(1, 0, 2)
    blocks = jnp.repeat(blocks, sharing, axis=0)
    w_heads = lax.all_to_all(blocks, "wide", 0, 0, tiled=True).reshape(model_width, 3 * width)
    w_out_heads = w_out
    if sharing > 1:
        near = [list(range(a, a + sharing)) for a in range(0, size, sharing)]
        w_out_heads = lax.all_gather(w_out, "wide", axis=0, tiled=True, axis_index_groups=near)

    factor_one = rms_factor(inputs)
    normed_one = inputs * factor_one
    norm_one = (normed_one * gain_one).astype(jnp.bfloat16)
    group_one = ring.gather(norm_one)
    lin = jnp.concatenate([dot_nn(rows, w_heads) for rows in group_one], axis=0)
    heads_attention, query, key, value, logs = attention_forward(
        slot_of, lengths, lin, cosine, sine
    )
    attention = own_columns(heads_attention)
    starts = [0]
    for rows in group_one:
        starts.append(starts[-1] + rows.shape[0])

    def group_of(array, step):
        return array[starts[step] : starts[step + 1]]

    def residual_part(step):
        mine, other = halves(group_of(attention, step))
        return dot_nn(mine, w_out), dot_nn(other, w_out)

    residual = inputs + ring.scatter(residual_part)
    factor_two = rms_factor(residual)
    normed_two = residual * factor_two
    norm_two = (normed_two * gain_two).astype(jnp.bfloat16)
    group_back = ring.gather(mlp_back)
    group_two = ring.gather(norm_two)
    w_both = jnp.concatenate([w_gate, w_up], axis=0)
    units = w_gate.shape[0]
    hidden = []
    both_back = []
    for rows, back in zip(group_two, group_back):
        both = dot_nt(rows, w_both)
        gate_proj, up_proj = both[:, :units], both[:, units:]
        hidden.append((jax.nn.silu(gate_proj) * up_proj).astype(jnp.bfloat16))
        both_back.append(
            jnp.concatenate(swiglu_back(dot_nt(back, w_down), gate_proj, up_proj), axis=1)
        )

    def pull_part(step):
        mine, other = halves(both_back[step])
        return dot_nn(mine, w_both), dot_nn(other, w_both)

    def mlp_part(step):
        mine, other = halves(hidden[step])
        return dot_nn(mine, w_down), dot_nn(other, w_down)

    norm_two_back = ring.scatter(pull_part)
    residual_back = y_back + norm_back(norm_two_back, normed_two, gain_two, factor_two)
    gain_two_term = jnp.sum(norm_two_back * normed_two, axis=0)
    branch_back = residual_back.astype(jnp.bfloat16)
    group_branch = ring.gather(branch_back)
    upstream = jnp.concatenate(
        [dot_nt(rows, w_out_heads).astype(jnp.bfloat16) for rows in group_branch], axis=0
    )
    mlp_out = ring.scatter(mlp_part)
    block_output = (residual + mlp_out).astype(jnp.bfloat16)

    all_two = jnp.concatenate(group_two, axis=0)
    both_sum = both_sequences(contract_rows(jnp.concatenate(both_back, axis=0), all_two))
    down_sum = both_sequences(
        contract_rows(jnp.concatenate(hidden, axis=0), jnp.concatenate(group_back, axis=0))
    )
    out_sum = both_sequences(contract_rows(attention, jnp.concatenate(group_branch, axis=0)))

    lin_back = own_columns(
        attention_backward(
            slot_of, lengths, query, key, value, heads_attention, upstream, logs, cosine, sine
        )
    )
    w_own = own_columns(w_heads)

    def input_part(step):
        mine, other = halves(group_of(lin_back, step))
        return dot_nt(mine, w_own), dot_nt(other, w_own)

    heads_part = contract_rows(jnp.concatenate(group_one, axis=0), lin_back)
    gain_one_term = jnp.sum(heads_part * w_own.astype(jnp.float32), axis=1) / gain_one
    gain_totals = ring.total(jnp.stack([gain_one_term, gain_two_term]))
    heads_sum = both_sequences(heads_part).astype(jnp.bfloat16).reshape(size, own_width, 3 * own_width)
    heads_sum = lax.all_to_all(heads_sum, "wide", 0, 0, tiled=True).astype(jnp.float32)
    attention_sums = [
        heads_sum[:, :, piece * own_width : (piece + 1) * own_width]
        .transpose(1, 0, 2)
        .reshape(own_width, model_width)
        for piece in range(3)
    ]
    norm_one_back = ring.scatter(input_part)
    input_back = residual_back + norm_back(norm_one_back, normed_one, gain_one, factor_one)
    return (
        block_output[None],
        input_back[None],
        gain_totals[0],
        attention_sums[0],
        attention_sums[1],
        attention_sums[2],
        out_sum,
        gain_totals[1],
        both_sum[:units],
        both_sum[units:],
        down_sum,
    )


def solution(mesh):
    placed = (
        P("narrow", "wide", None),
        P("narrow"),
        P(),
        P("wide", None),
        P("wide", None),
        P("wide", None),
        P("wide", None),
        P(),
        P("wide", None),
        P("wide", None),
        P("wide", None),
        P("narrow", "wide", None),
    )
    return jax.shard_map(
        functools.partial(shards, Ring(mesh.shape["wide"])),
        mesh=mesh,
        in_specs=placed,
        out_specs=(
            P("narrow", "wide", None),
            P("narrow", "wide", None),
            P(),
            P("wide", None),
            P("wide", None),
            P("wide", None),
            P("wide", None),
            P(),
            P("wide", None),
            P("wide", None),
            P("wide", None),
        ),
        check_vma=False,
    )
```

```python
import functools
import jax
import jax.numpy as jnp
from jax import lax
from jax.experimental import pallas as pl
from jax.experimental.pallas import tpu as pltpu
import math
import numpy as np
from jax.sharding import PartitionSpec as P

HEAD_DIM = 64
NEGATIVE = -1e30
VMEM_LIMIT = 56 * 1024 * 1024


def dot_nt(a, b):
    return lax.dot_general(a, b, (((1,), (1,)), ((), ())), preferred_element_type=jnp.float32)


def dot_nn(a, b):
    return lax.dot_general(a, b, (((1,), (0,)), ((), ())), preferred_element_type=jnp.float32)


def half_turn(tensor):
    width = tensor.shape[-1]
    half_dim = HEAD_DIM // 2
    lane = lax.broadcasted_iota(jnp.int32, tensor.shape, 1)
    return jnp.where(
        lane % HEAD_DIM < half_dim,
        -pltpu.roll(tensor, width - half_dim, 1),
        pltpu.roll(tensor, half_dim, 1),
    )


def head_lanes(block, head):
    lane = lax.broadcasted_iota(jnp.int32, block.shape, 1)
    return jnp.where(lane // HEAD_DIM == head, block, jnp.zeros_like(block))


def forward_kernel(
    slot_ref, length_ref, lin_ref, cos_ref, sin_ref,
    att_ref, query_ref, key_ref, value_ref, log_ref,
    turned, attn_nat,
):
    rows = query_ref.shape[0]
    width = query_ref.shape[1]
    heads = width // HEAD_DIM
    slots = slot_ref.shape[0]
    shard = rows // slots
    length = length_ref[0]
    scale = HEAD_DIM ** (-0.5)

    @pl.loop(0, slots)
    def _(place):
        source = pl.ds(pl.multiple_of(slot_ref[place] * shard, shard), shard)
        target = pl.ds(pl.multiple_of(place * shard, shard), shard)
        cosine = cos_ref[target, :]
        sine = sin_ref[target, :]
        query_lin = lin_ref[source, 0:width]
        key_lin = lin_ref[source, width : 2 * width]
        value_lin = lin_ref[source, 2 * width : 3 * width]
        query = (query_lin * cosine + half_turn(query_lin) * sine).astype(jnp.bfloat16)
        query_ref[target, :] = (query.astype(jnp.float32) * scale).astype(jnp.bfloat16)
        key_ref[target, :] = (key_lin * cosine + half_turn(key_lin) * sine).astype(jnp.bfloat16)
        value_ref[target, :] = value_lin.astype(jnp.bfloat16)
        turned[:, target] = value_lin.T.astype(jnp.bfloat16)

    block_q = min(512, rows)
    block_k = min(512, rows)

    @pl.loop(0, rows // block_q)
    def _(i):
        q_first = pl.multiple_of(i * block_q, block_q)
        query = query_ref[pl.ds(q_first, block_q), :]
        parts = [head_lanes(query, h) for h in range(heads)]
        q_pos = q_first + lax.broadcasted_iota(jnp.int32, (1, block_q), 1)
        limit = jnp.minimum(q_pos, length - 1)
        full = jnp.minimum(q_first, length) // block_k
        stop = (jnp.minimum(q_first + block_q, length) + block_k - 1) // block_k

        def step(j, state, masked):
            k_first = pl.multiple_of(j * block_k, block_k)
            key = key_ref[pl.ds(k_first, block_k), :]
            out = []
            if masked:
                k_pos = k_first + lax.broadcasted_iota(jnp.int32, (block_k, block_q), 0)
                allowed = k_pos <= limit
            for h in range(heads):
                best, total, acc = state[3 * h : 3 * h + 3]
                scores = dot_nt(key, parts[h])
                if masked:
                    scores = jnp.where(allowed, scores, NEGATIVE)
                new_best = jnp.maximum(best, jnp.max(scores, axis=0, keepdims=True))
                weight = jnp.exp(scores - new_best)
                shrink = jnp.exp(best - new_best)
                total = total * shrink + jnp.sum(weight, axis=0, keepdims=True)
                value_t = turned[h * HEAD_DIM : (h + 1) * HEAD_DIM, pl.ds(k_first, block_k)]
                acc = acc * shrink + dot_nn(value_t, weight.astype(jnp.bfloat16))
                out += [new_best, total, acc]
            return tuple(out)

        state = ()
        for h in range(heads):
            state += (
                jnp.full((1, block_q), NEGATIVE, jnp.float32),
                jnp.zeros((1, block_q), jnp.float32),
                jnp.zeros((HEAD_DIM, block_q), jnp.float32),
            )
        state = lax.fori_loop(0, full, functools.partial(step, masked=False), state)
        state = lax.fori_loop(full, stop, functools.partial(step, masked=True), state)
        for h in range(heads):
            best, total, acc = state[3 * h : 3 * h + 3]
            log_ref[h : h + 1, pl.ds(q_first, block_q)] = best + jnp.log(total)
        joined = jnp.concatenate([state[3 * h + 2] / state[3 * h + 1] for h in range(heads)], axis=0)
        attn_nat[pl.ds(q_first, block_q), :] = joined.T.astype(jnp.bfloat16)

    @pl.loop(0, slots)
    def _(place):
        source = pl.ds(pl.multiple_of(slot_ref[place] * shard, shard), shard)
        target = pl.ds(pl.multiple_of(place * shard, shard), shard)
        att_ref[source, :] = attn_nat[target, :]


def attention_forward(slot_of, length, lin, cosine, sine):
    rows, width = cosine.shape
    vmem = pl.BlockSpec(memory_space=pltpu.VMEM)
    smem = pl.BlockSpec(memory_space=pltpu.SMEM)
    half = jax.ShapeDtypeStruct((rows, width), jnp.bfloat16)
    return pl.pallas_call(
        forward_kernel,
        out_shape=(half, half, half, half, jax.ShapeDtypeStruct((8, rows), jnp.float32)),
        in_specs=[smem, smem, vmem, vmem, vmem],
        out_specs=(vmem,) * 5,
        scratch_shapes=[
            pltpu.VMEM((width, rows), jnp.bfloat16),
            pltpu.VMEM((rows, width), jnp.bfloat16),
        ],
        compiler_params=pltpu.CompilerParams(vmem_limit_bytes=VMEM_LIMIT),
        cost_estimate=pl.CostEstimate(
            flops=4 * rows * rows * width, bytes_accessed=24 * rows * width, transcendentals=rows * rows
        ),
        name="attention_forward",
    )(slot_of, length, lin, cosine, sine)


def backward_kernel(
    slot_ref, length_ref, query_ref, key_ref, value_ref, att_ref, up_ref, log_ref, cos_ref, sin_ref,
    out_ref,
    key_t, up_nat, delta, key_acc, value_acc, query_acc,
):
    rows = query_ref.shape[0]
    width = query_ref.shape[1]
    heads = width // HEAD_DIM
    slots = slot_ref.shape[0]
    shard = rows // slots
    length = length_ref[0]
    scale = HEAD_DIM ** (-0.5)
    key_acc[...] = jnp.zeros_like(key_acc)
    value_acc[...] = jnp.zeros_like(value_acc)

    @pl.loop(0, slots)
    def _(place):
        source = pl.ds(pl.multiple_of(slot_ref[place] * shard, shard), shard)
        target = pl.ds(pl.multiple_of(place * shard, shard), shard)
        upstream = up_ref[source, :]
        up_nat[target, :] = upstream
        product = (upstream.astype(jnp.float32) * att_ref[source, :].astype(jnp.float32)).T
        for h in range(heads):
            delta[h : h + 1, target] = jnp.sum(
                product[h * HEAD_DIM : (h + 1) * HEAD_DIM, :], axis=0, keepdims=True
            )
        key_t[:, target] = key_ref[target, :].astype(jnp.float32).T.astype(jnp.bfloat16)

    block_q = min(512, rows)
    block_k = min(512, rows)

    @pl.loop(0, rows // block_q)
    def _(i):
        q_first = pl.multiple_of(i * block_q, block_q)
        here = pl.ds(q_first, block_q)
        query = query_ref[here, :]
        upstream = up_nat[here, :]
        q_parts = [head_lanes(query, h) for h in range(heads)]
        u_parts = [head_lanes(upstream, h) for h in range(heads)]
        logs = [log_ref[h : h + 1, here] for h in range(heads)]
        deltas = [delta[h : h + 1, here] for h in range(heads)]
        q_pos = q_first + lax.broadcasted_iota(jnp.int32, (1, block_q), 1)
        limit = jnp.minimum(q_pos, length - 1)
        full = jnp.minimum(q_first, length) // block_k
        stop = (jnp.minimum(q_first + block_q, length) + block_k - 1) // block_k

        def step(j, state, masked):
            k_first = pl.multiple_of(j * block_k, block_k)
            there = pl.ds(k_first, block_k)
            key = key_ref[there, :]
            value = value_ref[there, :]
            if masked:
                k_pos = k_first + lax.broadcasted_iota(jnp.int32, (block_k, block_q), 0)
                allowed = k_pos <= limit
            out = []
            key_add = None
            for h in range(heads):
                prob = jnp.exp(dot_nt(key, q_parts[h]) - logs[h])
                if masked:
                    prob = jnp.where(allowed, prob, 0.0)
                pulled = dot_nt(value, u_parts[h])
                score_back = (prob * (pulled - deltas[h])).astype(jnp.bfloat16)
                one = dot_nn(prob.astype(jnp.bfloat16), u_parts[h])
                two = dot_nn(score_back, q_parts[h])
                value_add = one if key_add is None else value_add + one
                key_add = two if key_add is None else key_add + two
                out.append(
                    state[h] + dot_nn(key_t[h * HEAD_DIM : (h + 1) * HEAD_DIM, there], score_back)
                )
            value_acc[there, :] += value_add
            key_acc[there, :] += key_add
            return tuple(out)

        state = tuple(jnp.zeros((HEAD_DIM, block_q), jnp.float32) for h in range(heads))
        state = lax.fori_loop(0, full, functools.partial(step, masked=False), state)
        state = lax.fori_loop(full, stop, functools.partial(step, masked=True), state)
        query_acc[here, :] = (jnp.concatenate(state, axis=0) * scale).T

    @pl.loop(0, slots)
    def _(place):
        source = pl.ds(pl.multiple_of(slot_ref[place] * shard, shard), shard)
        target = pl.ds(pl.multiple_of(place * shard, shard), shard)
        cosine = cos_ref[target, :]
        sine = sin_ref[target, :]
        for piece, held in enumerate((query_acc, key_acc)):
            grad = held[target, :]
            out_ref[source, piece * width : (piece + 1) * width] = (
                grad * cosine - half_turn(grad * sine)
            ).astype(jnp.bfloat16)
        out_ref[source, 2 * width : 3 * width] = value_acc[target, :].astype(jnp.bfloat16)


def attention_backward(slot_of, length, query, key, value, att, upstream, logs, cosine, sine):
    rows, width = query.shape
    vmem = pl.BlockSpec(memory_space=pltpu.VMEM)
    smem = pl.BlockSpec(memory_space=pltpu.SMEM)
    return pl.pallas_call(
        backward_kernel,
        out_shape=jax.ShapeDtypeStruct((rows, 3 * width), jnp.bfloat16),
        in_specs=[smem, smem] + [vmem] * 8,
        out_specs=vmem,
        scratch_shapes=[
            pltpu.VMEM((width, rows), jnp.bfloat16),
            pltpu.VMEM((rows, width), jnp.bfloat16),
            pltpu.VMEM((8, rows), jnp.float32),
            pltpu.VMEM((rows, width), jnp.float32),
            pltpu.VMEM((rows, width), jnp.float32),
            pltpu.VMEM((rows, width), jnp.float32),
        ],
        compiler_params=pltpu.CompilerParams(vmem_limit_bytes=VMEM_LIMIT),
        cost_estimate=pl.CostEstimate(
            flops=10 * rows * rows * width, bytes_accessed=36 * rows * width, transcendentals=rows * rows
        ),
        name="attention_backward",
    )(slot_of, length, query, key, value, att, upstream, logs, cosine, sine)


EPSILON = 1e-05
THETA = 130000.0


def contract_rows(left_side, right_side):
    return lax.dot_general(
        left_side, right_side, (((0,), (0,)), ((), ())), preferred_element_type=jnp.float32
    )


def rotary_tables(row_count, width):
    half_dim = HEAD_DIM // 2
    feature = (jnp.arange(width, dtype=jnp.int32) % half_dim).astype(jnp.float32)
    frequency = THETA ** (-feature * 2.0 / HEAD_DIM)
    angles = jnp.arange(row_count, dtype=jnp.float32)[:, None] * frequency[None, :]
    return (jnp.cos(angles), jnp.sin(angles))


def rms_factor(matrix):
    return lax.rsqrt(jnp.mean(matrix * matrix, axis=-1, keepdims=True) + EPSILON)


def norm_back(upstream, normed, gain_vec, factor):
    scaled = upstream * gain_vec
    return factor * (scaled - normed * jnp.mean(scaled * normed, axis=-1, keepdims=True))


def swiglu_back(hidden_back, gate_proj, up_proj):
    sigmoid_gate = jax.nn.sigmoid(gate_proj)
    gate_back = hidden_back * up_proj * sigmoid_gate * (1.0 + gate_proj * (1.0 - sigmoid_gate))
    up_back = hidden_back * jax.nn.silu(gate_proj)
    return (gate_back.astype(jnp.bfloat16), up_back.astype(jnp.bfloat16))


SMALL = pl.CostEstimate(flops=1024, bytes_accessed=1024, transcendentals=0)


def dot_tn(a, b):
    return lax.dot_general(a, b, (((0,), (0,)), ((), ())), preferred_element_type=jnp.float32)


def fitting(tile, extent):
    return math.gcd(tile, extent)


def call_kernel(body, name, grid, ins, outs, args):
    return pl.pallas_call(
        body,
        grid=grid,
        in_specs=[pl.BlockSpec(*spec) for spec in ins],
        out_specs=[pl.BlockSpec(block, index) for block, index, _, _ in outs],
        out_shape=[jax.ShapeDtypeStruct(shape, dtype) for _, _, shape, dtype in outs],
        compiler_params=pltpu.CompilerParams(vmem_limit_bytes=VMEM_LIMIT),
        cost_estimate=SMALL,
        name=name,
    )(*args)


def first(i):
    return (0, 0)


def along(i):
    return (0, i)


def down_rows(i):
    return (i, 0)


def fill(target_ref, piece_refs):
    start = 0
    for piece_ref in piece_refs:
        count = piece_ref.shape[0]
        target_ref[start : start + count, :] = piece_ref[...]
        start += count


def grads_kernel(lefts, rights, *refs):
    out_refs, (left_ref, right_ref) = refs[lefts + rights : -2], refs[-2:]

    @pl.when(pl.program_id(0) == 0)
    def _():
        fill(left_ref, refs[:lefts])

    fill(right_ref, refs[lefts : lefts + rights])
    total = dot_tn(left_ref[...], right_ref[...]).astype(jnp.bfloat16)
    rows = out_refs[0].shape[0]
    for piece, out_ref in enumerate(out_refs):
        out_ref[...] = total[piece * rows : (piece + 1) * rows]


def weight_grads(lefts, rights, rows):
    count = sum(piece.shape[0] for piece in lefts)
    wide = lefts[0].shape[1]
    width = rights[0].shape[1]
    tile = fitting(512, width)
    return pl.pallas_call(
        functools.partial(grads_kernel, len(lefts), len(rights)),
        grid=(width // tile,),
        in_specs=[pl.BlockSpec(piece.shape, first) for piece in lefts]
        + [pl.BlockSpec((piece.shape[0], tile), along) for piece in rights],
        out_specs=[pl.BlockSpec((rows, tile), along)] * (wide // rows),
        out_shape=[jax.ShapeDtypeStruct((rows, width), jnp.bfloat16)] * (wide // rows),
        scratch_shapes=[
            pltpu.VMEM((count, wide), jnp.bfloat16),
            pltpu.VMEM((count, tile), jnp.bfloat16),
        ],
        compiler_params=pltpu.CompilerParams(vmem_limit_bytes=VMEM_LIMIT),
        cost_estimate=SMALL,
        name="weight_grads",
    )(*lefts, *rights)


def heads_kernel(upper_ref, left_ref, right_ref, weight_ref, keep_ref, give_ref, gain_ref):
    total = dot_tn(left_ref[...], right_ref[...])
    count, half, width = keep_ref.shape
    sums = jnp.sum(total * weight_ref[...].astype(jnp.float32), axis=1, keepdims=True)
    gain_ref[...] = jnp.broadcast_to(sums, (total.shape[0], 128)).T[:1]
    blocks = total.astype(jnp.bfloat16).reshape(count, 2, half, width)
    upper = upper_ref[0] == 1
    keep_ref[...] = jnp.where(upper, blocks[:, 1], blocks[:, 0])
    give_ref[...] = jnp.where(upper, blocks[:, 0], blocks[:, 1])


def heads_grads(left, right, weight, upper, rows):
    count, wide = left.shape
    width = right.shape[1]
    tile = fitting(512, wide)
    half = ((tile // rows, rows // 2, width), lambda i: (i, 0, 0))
    whole = ((wide // rows, rows // 2, width), jnp.bfloat16)
    return pl.pallas_call(
        heads_kernel,
        grid=(wide // tile,),
        in_specs=[
            pl.BlockSpec(memory_space=pltpu.SMEM),
            pl.BlockSpec((count, tile), along),
            pl.BlockSpec((count, width), first),
            pl.BlockSpec((tile, width), down_rows),
        ],
        out_specs=[pl.BlockSpec(*half), pl.BlockSpec(*half), pl.BlockSpec((1, tile), along)],
        out_shape=[
            jax.ShapeDtypeStruct(*whole),
            jax.ShapeDtypeStruct(*whole),
            jax.ShapeDtypeStruct((1, wide), jnp.float32),
        ],
        compiler_params=pltpu.CompilerParams(vmem_limit_bytes=VMEM_LIMIT),
        cost_estimate=SMALL,
        name="heads_grads",
    )(upper, left, right, weight)


def assemble_kernel(side_ref, near_ref, far_ref, *out_refs):
    half, width = near_ref.shape[1:]
    columns = width // len(out_refs)
    upper = side_ref[0] == 1
    low = jnp.where(upper, far_ref[...], near_ref[...]).astype(jnp.float32)
    high = jnp.where(upper, near_ref[...], far_ref[...]).astype(jnp.float32)
    for piece, out_ref in enumerate(out_refs):
        for source in range(near_ref.shape[0]):
            place = slice(source * columns, (source + 1) * columns)
            taken = slice(piece * columns, (piece + 1) * columns)
            out_ref[:half, place] = low[source, :, taken]
            out_ref[half:, place] = high[source, :, taken]


def assemble(near, far, side, count):
    size, half, width = near.shape
    shape = (2 * half, size * width // count)
    vmem = pl.BlockSpec(memory_space=pltpu.VMEM)
    return pl.pallas_call(
        assemble_kernel,
        in_specs=[pl.BlockSpec(memory_space=pltpu.SMEM), vmem, vmem],
        out_specs=[vmem] * count,
        out_shape=[jax.ShapeDtypeStruct(shape, jnp.float32)] * count,
        compiler_params=pltpu.CompilerParams(vmem_limit_bytes=VMEM_LIMIT),
        cost_estimate=SMALL,
        name="assemble",
    )(side, near, far)


def sums_kernel(*refs):
    out_ref = refs[-1]
    count = (len(refs) - 1) // 2
    rows = refs[0].shape[0]
    for piece in range(count):
        out_ref[piece * rows : (piece + 1) * rows, :] = refs[piece][...].astype(
            jnp.float32
        ) + refs[count + piece][...].astype(jnp.float32)


def sum_pieces(parts, others):
    rows, width = parts[0].shape
    tile = fitting(512, width)
    total = rows * len(parts)
    return call_kernel(
        sums_kernel,
        "sum_pieces",
        (width // tile,),
        [((rows, tile), along)] * (2 * len(parts)),
        [((total, tile), along, (total, width), jnp.float32)],
        (*parts, *others),
    )


class Ring:
    def __init__(self, size):
        self.size = size
        self.pairs = size // 2
        self.reach = self.pairs // 2
        columns = self.pairs // 2
        self.order = [2 * a for a in range(columns)] + [2 * a + 1 for a in reversed(range(columns))]
        self.ahead = []
        self.behind = []
        for place, pair in enumerate(self.order):
            following = self.order[(place + 1) % self.pairs]
            for lane in range(2):
                self.ahead.append((2 * pair + lane, 2 * following + lane))
                self.behind.append((2 * following + lane, 2 * pair + lane))
        self.across = [(device, device ^ 1) for device in range(size)]

    def slots(self):
        offsets = [(0, 0), (0, 1)]
        for step in range(1, self.reach):
            offsets += [(-step, 0), (step, 0), (-step, 1), (step, 1)]
        offsets += [(self.reach, 0), (self.reach, 1)]
        table = np.zeros((self.size, self.size), np.int32)
        for device in range(self.size):
            place = self.order.index(device // 2)
            for slot, (offset, flip) in enumerate(offsets):
                pair = self.order[(place + offset) % self.pairs]
                table[device, 2 * pair + (device % 2 ^ flip)] = slot
        return table

    def forward(self, array):
        return lax.ppermute(array, "wide", self.ahead)

    def backward(self, array):
        return lax.ppermute(array, "wide", self.behind)

    def twin(self, array):
        return lax.ppermute(array, "wide", self.across)

    def gather(self, rows, groups):
        groups.append([rows, self.twin(rows)])
        ahead = behind = rows
        middle = rows.shape[0] // 2
        for step in range(1, self.reach + 1):
            if step == self.reach:
                ahead, behind = ahead[:middle], behind[middle:]
            (ahead, behind), _ = yield ((self.forward, ahead), (self.backward, behind)), ()
            groups.append([ahead, behind, self.twin(ahead), self.twin(behind)])

    def scatter(self, make):
        down = up = None
        held = ()
        for step in range(self.reach, -1, -1):
            mine, other = make(step, *held)
            total = mine + self.twin(other.astype(jnp.bfloat16)).astype(jnp.float32)
            count = total.shape[0] // 2
            if step == 0:
                return total + down.astype(jnp.float32) + up.astype(jnp.float32)
            low, high = total[:count], total[count:]
            if step == self.reach - 1:
                middle = count // 2
                low = jnp.concatenate([low[:middle] + down.astype(jnp.float32), low[middle:]], axis=0)
                high = jnp.concatenate([high[:middle], high[middle:] + up.astype(jnp.float32)], axis=0)
            elif step < self.reach - 1:
                low = low + down.astype(jnp.float32)
                high = high + up.astype(jnp.float32)
            held = (low.astype(jnp.bfloat16), high.astype(jnp.bfloat16))
            (down, up), _ = yield ((self.backward, held[0]), (self.forward, held[1])), ()

    def total(self, array):
        bit = 1
        while bit < self.size:
            pairs = [(i, i ^ bit) for i in range(self.size)]
            send = functools.partial(lax.ppermute, axis_name="wide", perm=pairs)
            ((other,), _) = yield ((send, array),), ()
            array = array + other
            bit *= 2
        ((other,), _) = yield ((swapped, array),), ()
        return array + other


class Stream:
    def __init__(self, hops):
        self.hops = hops
        self.asked, self.beside = next(hops)
        self.result = None

    def post(self):
        return [send(array) for send, array in self.asked]

    def land(self, arrived, beside):
        try:
            self.asked, self.beside = self.hops.send((arrived, beside))
        except StopIteration as end:
            self.asked, self.beside = None, ()
            self.result = end.value


class Swaps:
    def __init__(self):
        self.waiting = []
        self.done = {}
        self.parts = {}

    def add(self, name, parts):
        self.parts[name] = list(parts)
        self.done[name] = []
        self.waiting += [(name, index) for index in range(len(parts))]

    def sums(self, name):
        return (self.parts[name], self.done[name])


def joined(*lists):
    held = list(lax.optimization_barrier(tuple(array for part in lists for array in part)))
    result = []
    for part in lists:
        result.append(held[: len(part)])
        held = held[len(part) :]
    return result


def hop(streams, swaps=None, count=1, beside=(), work=None, given=()):
    streams = [stream for stream in streams if stream.asked is not None]
    ready = []
    if swaps is not None:
        ready, swaps.waiting = swaps.waiting[:count], swaps.waiting[count:]
    if work is not None:
        flat, tree = jax.tree.flatten(given)
        *sent, flat = joined(*[[array for _, array in s.asked] for s in streams], flat)
        for stream, arrays in zip(streams, sent):
            stream.asked = [(send, array) for (send, _), array in zip(stream.asked, arrays)]
        beside = work(*jax.tree.unflatten(tree, flat))
    lists = [stream.post() for stream in streams]
    lists += [stream.beside for stream in streams]
    lists.append([swapped(swaps.parts[name][index]) for name, index in ready])
    lists.append(beside)
    *lists, moved, beside = joined(*lists)
    for (name, _), piece in zip(ready, moved):
        swaps.done[name].append(piece)
    for place, stream in enumerate(streams):
        stream.land(lists[place], lists[len(streams) + place])
    return beside


def travel(stream, swaps=None, count=1):
    while stream.asked is not None:
        hop([stream], swaps, count)
    return stream.result


def swapped(part):
    return lax.ppermute(part, "narrow", [(0, 1), (1, 0)])


def after(array, *others):
    return lax.optimization_barrier((array,) + others)[0]


def halves(array):
    middle = array.shape[0] // 2
    return array[:middle], array[middle:]


def shards(
    ring,
    layer_input,
    lengths,
    attn_gain,
    w_query,
    w_key,
    w_value,
    w_out,
    mlp_gain,
    w_gate,
    w_up,
    w_down,
    cotangent,
):
    size = ring.size
    local_rows = layer_input.shape[1]
    model_width = layer_input.shape[2]
    row_count = local_rows * size
    own_width = model_width // size
    width = max(own_width, 2 * HEAD_DIM)
    sharing = width // own_width
    device = lax.axis_index("wide")
    member = device % sharing
    slot_of = lax.dynamic_index_in_dim(jnp.asarray(ring.slots()), device, keepdims=False)

    def own_columns(array):
        if sharing == 1:
            return array
        runs = array.reshape(array.shape[0], -1, sharing, own_width)
        return lax.dynamic_index_in_dim(runs, member, axis=2, keepdims=False).reshape(
            array.shape[0], -1
        )

    positions = device * local_rows + jnp.arange(local_rows, dtype=jnp.int32)
    valid_rows = (positions < lengths[0]).astype(jnp.float32)[:, None]
    cosine, sine = rotary_tables(row_count, width)
    inputs = layer_input[0].astype(jnp.float32)
    gain_one = attn_gain.astype(jnp.float32)
    gain_two = mlp_gain.astype(jnp.float32)
    y_back = cotangent[0].astype(jnp.float32) * valid_rows
    mlp_back = y_back.astype(jnp.bfloat16)

    blocks = jnp.concatenate(
        [w.reshape(own_width, -1, width) for w in (w_query, w_key, w_value)], axis=-1
    ).transpose(1, 0, 2)
    blocks = jnp.repeat(blocks, sharing, axis=0)
    half_rows = own_width // 2
    upper = lax.axis_index("narrow") == 1
    w_out_heads = w_out
    if sharing > 1:
        near = [list(range(a, a + sharing)) for a in range(0, size, sharing)]
        w_out_heads = lax.all_gather(w_out, "wide", axis=0, tiled=True, axis_index_groups=near)
    units = w_gate.shape[0]
    w_both = jnp.concatenate([w_gate, w_up], axis=0)
    factor_one = rms_factor(inputs)
    normed_one = inputs * factor_one
    norm_one = (normed_one * gain_one).astype(jnp.bfloat16)
    sent = jnp.where(upper, blocks[:, half_rows:], blocks[:, :half_rows])
    near_half = lax.all_to_all(after(sent, norm_one), "wide", 0, 0, tiled=True)
    group_one = []
    one = Stream(ring.gather(norm_one, group_one))
    hop([one])
    cosine, sine = hop([one], beside=(cosine, sine))
    travel(one)
    far_half = swapped(near_half)
    w_heads = jnp.stack(
        [jnp.where(upper, far_half, near_half), jnp.where(upper, near_half, far_half)], axis=1
    ).reshape(model_width, 3 * width)
    all_one = jnp.concatenate(sum(group_one, []), axis=0)
    lin = dot_nn(all_one, w_heads)
    starts = [0]
    for rows in group_one:
        starts.append(starts[-1] + sum(piece.shape[0] for piece in rows))

    def group_of(array, step):
        return array[starts[step] : starts[step + 1]]

    group_back = []
    back = Stream(ring.gather(after(mlp_back, lin), group_back))
    heads_attention, query, key, value, logs = hop(
        [back], beside=attention_forward(slot_of, lengths, lin, cosine, sine)
    )
    attention = own_columns(heads_attention)

    def residual_part(step, *held):
        mine, other = halves(group_of(attention, step))
        return dot_nn(mine, w_out), dot_nn(other, w_out)

    mixed = Stream(ring.scatter(residual_part))
    while mixed.asked is not None:
        hop([mixed, back])
    residual = inputs + mixed.result
    factor_two = rms_factor(residual)
    normed_two = residual * factor_two
    norm_two = (normed_two * gain_two).astype(jnp.bfloat16)
    group_two = []
    two = Stream(ring.gather(norm_two, group_two))
    hidden = []
    both_back = []

    def feed(step):
        both = dot_nt(jnp.concatenate(group_two[step], axis=0), w_both)
        gate_proj, up_proj = both[:, :units], both[:, units:]
        hidden_back = dot_nt(jnp.concatenate(group_back[step], axis=0), w_down)
        return (
            (jax.nn.silu(gate_proj) * up_proj).astype(jnp.bfloat16),
            jnp.concatenate(swiglu_back(hidden_back, gate_proj, up_proj), axis=1),
        )

    hop([two])
    for step in range(1, ring.reach):
        fed = hop([two], beside=feed(step - 1))
        hidden.append(fed[0])
        both_back.append(fed[1])
    for step in (ring.reach - 1, ring.reach):
        fed = feed(step)
        hidden.append(fed[0])
        both_back.append(fed[1])

    def pull_part(step, *held):
        mine, other = halves(after(both_back[step], *held))
        return dot_nn(mine, w_both), dot_nn(other, w_both)

    def mlp_part(step, *held):
        mine, other = halves(after(hidden[step], *held))
        return dot_nn(mine, w_down), dot_nn(other, w_down)

    swaps = Swaps()
    grads = functools.partial(weight_grads, rows=local_rows)
    pull = Stream(ring.scatter(pull_part))
    hop([pull])
    down_parts = hop([pull], work=grads, given=(hidden, sum(group_back, [])))
    swaps.add("down", down_parts)
    norm_two_back = travel(pull, swaps)
    residual_back = y_back + norm_back(norm_two_back, normed_two, gain_two, factor_two)
    gain_two_term = jnp.sum(norm_two_back * normed_two, axis=0)
    branch_back = residual_back.astype(jnp.bfloat16)
    mlp = Stream(ring.scatter(mlp_part))
    group_branch = []
    branch = Stream(ring.gather(branch_back, group_branch))
    pieces_two = sum(group_two, [])
    for name, place in (("gate", slice(None, units)), ("up", slice(units, None))):
        parts = hop(
            [branch, mlp],
            swaps,
            2,
            work=grads,
            given=([both[:, place] for both in both_back], pieces_two),
        )
        swaps.add(name, parts)
    (down_sum,) = hop([branch], swaps, work=sum_pieces, given=swaps.sums("down"))
    while branch.asked is not None:
        hop([branch], swaps)
    upstream = jnp.concatenate(
        [
            dot_nt(jnp.concatenate(rows, axis=0), w_out_heads).astype(jnp.bfloat16)
            for rows in group_branch
        ],
        axis=0,
    )
    (lin_back,) = hop(
        [mlp],
        swaps,
        2,
        beside=(
            attention_backward(
                slot_of, lengths, query, key, value, heads_attention, upstream, logs, cosine, sine
            ),
        ),
    )
    lin_back = own_columns(lin_back)
    w_own = own_columns(w_heads)

    def input_part(step, *held):
        mine, other = halves(after(group_of(lin_back, step), *held))
        return dot_nt(mine, w_own), dot_nt(other, w_own)

    pulled = Stream(ring.scatter(input_part))
    side = lax.axis_index("narrow").reshape(1)
    keep, give, gain_one_sum = hop(
        [mlp],
        swaps,
        work=functools.partial(heads_grads, rows=own_width),
        given=(all_one, lin_back, w_own, side),
    )
    while mlp.asked is not None:
        hop([mlp], swaps)
    block_output = (residual + mlp.result).astype(jnp.bfloat16)
    totals = Stream(ring.total(jnp.stack([gain_one_sum[0] / gain_one, gain_two_term])))
    hop([totals])

    def before(piece, parts, others):
        return (swapped(piece), *sum_pieces(parts, others))

    given, gate_sum = hop([pulled, totals], work=before, given=(give, *swaps.sums("gate")))
    heads_sum = lax.all_to_all(
        (keep.astype(jnp.float32) + given.astype(jnp.float32)).astype(jnp.bfloat16),
        "wide",
        0,
        0,
        tiled=True,
    )
    out_parts = hop(
        [pulled, totals],
        swaps,
        work=functools.partial(weight_grads, rows=own_width),
        given=([attention], sum(group_branch, [])),
    )
    while swaps.waiting:
        hop([], swaps)
    swaps.add("out", out_parts)
    (up_sum,) = hop([pulled, totals], swaps, work=sum_pieces, given=swaps.sums("up"))
    far, out_sum = hop([pulled, totals], work=before, given=(heads_sum, *swaps.sums("out")))
    while pulled.asked is not None or totals.asked is not None:
        hop([pulled, totals])
    norm_one_back = pulled.result
    gain_totals = totals.result
    attention_sums = assemble(heads_sum, far, side, 3)
    input_back = residual_back + norm_back(norm_one_back, normed_one, gain_one, factor_one)
    return (
        block_output[None],
        input_back[None],
        gain_totals[0],
        attention_sums[0],
        attention_sums[1],
        attention_sums[2],
        out_sum,
        gain_totals[1],
        gate_sum,
        up_sum,
        down_sum,
    )


def solution(mesh):
    placed = (
        P("narrow", "wide", None),
        P("narrow"),
        P(),
        P("wide", None),
        P("wide", None),
        P("wide", None),
        P("wide", None),
        P(),
        P("wide", None),
        P("wide", None),
        P("wide", None),
        P("narrow", "wide", None),
    )
    return jax.shard_map(
        functools.partial(shards, Ring(mesh.shape["wide"])),
        mesh=mesh,
        in_specs=placed,
        out_specs=(
            P("narrow", "wide", None),
            P("narrow", "wide", None),
            P(),
            P("wide", None),
            P("wide", None),
            P("wide", None),
            P("wide", None),
            P(),
            P("wide", None),
            P("wide", None),
            P("wide", None),
        ),
        check_vma=False,
    )
```

```python
import functools
import jax
import jax.numpy as jnp
from jax import lax
from jax.experimental import pallas as pl
from jax.experimental.pallas import tpu as pltpu
import math
import numpy as np
from jax.sharding import PartitionSpec as P

HEAD_DIM = 64
NEGATIVE = -1e30
VMEM_LIMIT = 56 * 1024 * 1024


def dot_nt(a, b):
    return lax.dot_general(a, b, (((1,), (1,)), ((), ())), preferred_element_type=jnp.float32)


def dot_nn(a, b):
    return lax.dot_general(a, b, (((1,), (0,)), ((), ())), preferred_element_type=jnp.float32)


def half_turn(tensor):
    width = tensor.shape[-1]
    half_dim = HEAD_DIM // 2
    lane = lax.broadcasted_iota(jnp.int32, tensor.shape, 1)
    return jnp.where(
        lane % HEAD_DIM < half_dim,
        -pltpu.roll(tensor, width - half_dim, 1),
        pltpu.roll(tensor, half_dim, 1),
    )


def head_lanes(block, head):
    lane = lax.broadcasted_iota(jnp.int32, block.shape, 1)
    return jnp.where(lane // HEAD_DIM == head, block, jnp.zeros_like(block))


def forward_kernel(
    slot_ref, length_ref, lin_ref, cos_ref, sin_ref,
    att_ref, query_ref, key_ref, value_ref, log_ref,
    turned, attn_nat,
):
    rows = query_ref.shape[0]
    width = query_ref.shape[1]
    heads = width // HEAD_DIM
    slots = slot_ref.shape[0]
    shard = rows // slots
    length = length_ref[0]
    scale = HEAD_DIM ** (-0.5)

    @pl.loop(0, slots, unroll=4)
    def _(place):
        source = pl.ds(pl.multiple_of(slot_ref[place] * shard, shard), shard)
        target = pl.ds(pl.multiple_of(place * shard, shard), shard)
        cosine = cos_ref[target, :]
        sine = sin_ref[target, :]
        query_lin = lin_ref[source, 0:width]
        key_lin = lin_ref[source, width : 2 * width]
        value_lin = lin_ref[source, 2 * width : 3 * width]
        query = (query_lin * cosine + half_turn(query_lin) * sine).astype(jnp.bfloat16)
        query_ref[target, :] = (query.astype(jnp.float32) * scale).astype(jnp.bfloat16)
        key_ref[target, :] = (key_lin * cosine + half_turn(key_lin) * sine).astype(jnp.bfloat16)
        value_ref[target, :] = value_lin.astype(jnp.bfloat16)
        turned[:, target] = value_lin.T.astype(jnp.bfloat16)

    block_q = min(1024, rows)
    block_k = min(512, rows)

    @pl.loop(0, rows // block_q)
    def _(i):
        q_first = pl.multiple_of(i * block_q, block_q)
        query = query_ref[pl.ds(q_first, block_q), :]
        parts = [head_lanes(query, h) for h in range(heads)]
        q_pos = q_first + lax.broadcasted_iota(jnp.int32, (1, block_q), 1)
        limit = jnp.minimum(q_pos, length - 1)
        full = jnp.minimum(q_first, length) // block_k
        stop = (jnp.minimum(q_first + block_q, length) + block_k - 1) // block_k

        def step(j, state, masked):
            k_first = pl.multiple_of(j * block_k, block_k)
            key = key_ref[pl.ds(k_first, block_k), :]
            out = []
            if masked:
                k_pos = k_first + lax.broadcasted_iota(jnp.int32, (block_k, block_q), 0)
                allowed = k_pos <= limit
            for h in range(heads):
                best, total, acc = state[3 * h : 3 * h + 3]
                scores = dot_nt(key, parts[h])
                if masked:
                    scores = jnp.where(allowed, scores, NEGATIVE)
                new_best = jnp.maximum(best, jnp.max(scores, axis=0, keepdims=True))
                weight = jnp.exp(scores - new_best)
                shrink = jnp.exp(best - new_best)
                total = total * shrink + jnp.sum(weight, axis=0, keepdims=True)
                value_t = turned[h * HEAD_DIM : (h + 1) * HEAD_DIM, pl.ds(k_first, block_k)]
                acc = acc * shrink + dot_nn(value_t, weight.astype(jnp.bfloat16))
                out += [new_best, total, acc]
            return tuple(out)

        state = ()
        for h in range(heads):
            state += (
                jnp.full((1, block_q), NEGATIVE, jnp.float32),
                jnp.zeros((1, block_q), jnp.float32),
                jnp.zeros((HEAD_DIM, block_q), jnp.float32),
            )
        state = lax.fori_loop(0, full, functools.partial(step, masked=False), state)
        state = lax.fori_loop(full, stop, functools.partial(step, masked=True), state)
        for h in range(heads):
            best, total, acc = state[3 * h : 3 * h + 3]
            log_ref[h : h + 1, pl.ds(q_first, block_q)] = best + jnp.log(total)
        joined = jnp.concatenate([state[3 * h + 2] / state[3 * h + 1] for h in range(heads)], axis=0)
        attn_nat[pl.ds(q_first, block_q), :] = joined.T.astype(jnp.bfloat16)

    @pl.loop(0, slots, unroll=4)
    def _(place):
        source = pl.ds(pl.multiple_of(slot_ref[place] * shard, shard), shard)
        target = pl.ds(pl.multiple_of(place * shard, shard), shard)
        att_ref[source, :] = attn_nat[target, :]


def attention_forward(slot_of, length, lin, cosine, sine):
    rows, width = cosine.shape
    vmem = pl.BlockSpec(memory_space=pltpu.VMEM)
    smem = pl.BlockSpec(memory_space=pltpu.SMEM)
    half = jax.ShapeDtypeStruct((rows, width), jnp.bfloat16)
    return pl.pallas_call(
        forward_kernel,
        out_shape=(half, half, half, half, jax.ShapeDtypeStruct((8, rows), jnp.float32)),
        in_specs=[smem, smem, vmem, vmem, vmem],
        out_specs=(vmem,) * 5,
        scratch_shapes=[
            pltpu.VMEM((width, rows), jnp.bfloat16),
            pltpu.VMEM((rows, width), jnp.bfloat16),
        ],
        compiler_params=pltpu.CompilerParams(vmem_limit_bytes=VMEM_LIMIT),
        cost_estimate=pl.CostEstimate(
            flops=4 * rows * rows * width, bytes_accessed=24 * rows * width, transcendentals=rows * rows
        ),
        name="attention_forward",
    )(slot_of, length, lin, cosine, sine)


def backward_kernel(
    slot_ref, length_ref, query_ref, key_ref, value_ref, att_ref, up_ref, log_ref, cos_ref, sin_ref,
    out_ref,
    key_t, up_nat, delta, key_acc, value_acc, query_acc,
):
    rows = query_ref.shape[0]
    width = query_ref.shape[1]
    heads = width // HEAD_DIM
    slots = slot_ref.shape[0]
    shard = rows // slots
    length = length_ref[0]
    scale = HEAD_DIM ** (-0.5)
    key_acc[...] = jnp.zeros_like(key_acc)
    value_acc[...] = jnp.zeros_like(value_acc)

    @pl.loop(0, slots, unroll=4)
    def _(place):
        source = pl.ds(pl.multiple_of(slot_ref[place] * shard, shard), shard)
        target = pl.ds(pl.multiple_of(place * shard, shard), shard)
        upstream = up_ref[source, :]
        up_nat[target, :] = upstream
        product = (upstream.astype(jnp.float32) * att_ref[source, :].astype(jnp.float32)).T
        for h in range(heads):
            delta[h : h + 1, target] = jnp.sum(
                product[h * HEAD_DIM : (h + 1) * HEAD_DIM, :], axis=0, keepdims=True
            )
        key_t[:, target] = key_ref[target, :].astype(jnp.float32).T.astype(jnp.bfloat16)

    block_q = min(512, rows)
    block_k = min(512, rows)

    @pl.loop(0, rows // block_q)
    def _(i):
        q_first = pl.multiple_of(i * block_q, block_q)
        here = pl.ds(q_first, block_q)
        query = query_ref[here, :]
        upstream = up_nat[here, :]
        q_parts = [head_lanes(query, h) for h in range(heads)]
        u_parts = [head_lanes(upstream, h) for h in range(heads)]
        logs = [log_ref[h : h + 1, here] for h in range(heads)]
        deltas = [delta[h : h + 1, here] for h in range(heads)]
        q_pos = q_first + lax.broadcasted_iota(jnp.int32, (1, block_q), 1)
        limit = jnp.minimum(q_pos, length - 1)
        full = jnp.minimum(q_first, length) // block_k
        stop = (jnp.minimum(q_first + block_q, length) + block_k - 1) // block_k

        def step(j, state, masked):
            k_first = pl.multiple_of(j * block_k, block_k)
            there = pl.ds(k_first, block_k)
            key = key_ref[there, :]
            value = value_ref[there, :]
            if masked:
                k_pos = k_first + lax.broadcasted_iota(jnp.int32, (block_k, block_q), 0)
                allowed = k_pos <= limit
            out = []
            key_add = None
            for h in range(heads):
                prob = jnp.exp(dot_nt(key, q_parts[h]) - logs[h])
                if masked:
                    prob = jnp.where(allowed, prob, 0.0)
                pulled = dot_nt(value, u_parts[h])
                score_back = (prob * (pulled - deltas[h])).astype(jnp.bfloat16)
                one = dot_nn(prob.astype(jnp.bfloat16), u_parts[h])
                two = dot_nn(score_back, q_parts[h])
                value_add = one if key_add is None else value_add + one
                key_add = two if key_add is None else key_add + two
                out.append(
                    state[h] + dot_nn(key_t[h * HEAD_DIM : (h + 1) * HEAD_DIM, there], score_back)
                )
            value_acc[there, :] += value_add
            key_acc[there, :] += key_add
            return tuple(out)

        state = tuple(jnp.zeros((HEAD_DIM, block_q), jnp.float32) for h in range(heads))
        state = lax.fori_loop(0, full, functools.partial(step, masked=False), state)
        state = lax.fori_loop(full, stop, functools.partial(step, masked=True), state)
        query_acc[here, :] = (jnp.concatenate(state, axis=0) * scale).T

    @pl.loop(0, slots, unroll=4)
    def _(place):
        source = pl.ds(pl.multiple_of(slot_ref[place] * shard, shard), shard)
        target = pl.ds(pl.multiple_of(place * shard, shard), shard)
        cosine = cos_ref[target, :]
        sine = sin_ref[target, :]
        for piece, held in enumerate((query_acc, key_acc)):
            grad = held[target, :]
            out_ref[source, piece * width : (piece + 1) * width] = (
                grad * cosine - half_turn(grad * sine)
            ).astype(jnp.bfloat16)
        out_ref[source, 2 * width : 3 * width] = value_acc[target, :].astype(jnp.bfloat16)


def attention_backward(slot_of, length, query, key, value, att, upstream, logs, cosine, sine):
    rows, width = query.shape
    vmem = pl.BlockSpec(memory_space=pltpu.VMEM)
    smem = pl.BlockSpec(memory_space=pltpu.SMEM)
    return pl.pallas_call(
        backward_kernel,
        out_shape=[jax.ShapeDtypeStruct((rows, 3 * width), jnp.bfloat16)],
        in_specs=[smem, smem] + [vmem] * 8,
        out_specs=[vmem],
        scratch_shapes=[
            pltpu.VMEM((width, rows), jnp.bfloat16),
            pltpu.VMEM((rows, width), jnp.bfloat16),
            pltpu.VMEM((8, rows), jnp.float32),
            pltpu.VMEM((rows, width), jnp.float32),
            pltpu.VMEM((rows, width), jnp.float32),
            pltpu.VMEM((rows, width), jnp.float32),
        ],
        compiler_params=pltpu.CompilerParams(vmem_limit_bytes=VMEM_LIMIT),
        cost_estimate=pl.CostEstimate(
            flops=10 * rows * rows * width, bytes_accessed=36 * rows * width, transcendentals=rows * rows
        ),
        name="attention_backward",
    )(slot_of, length, query, key, value, att, upstream, logs, cosine, sine)


EPSILON = 1e-05
THETA = 130000.0


def contract_rows(left_side, right_side):
    return lax.dot_general(
        left_side, right_side, (((0,), (0,)), ((), ())), preferred_element_type=jnp.float32
    )


def rotary_tables(row_count, width):
    half_dim = HEAD_DIM // 2
    feature = (jnp.arange(width, dtype=jnp.int32) % half_dim).astype(jnp.float32)
    frequency = THETA ** (-feature * 2.0 / HEAD_DIM)
    angles = jnp.arange(row_count, dtype=jnp.float32)[:, None] * frequency[None, :]
    return (jnp.cos(angles), jnp.sin(angles))


def rms_factor(matrix):
    return lax.rsqrt(jnp.mean(matrix * matrix, axis=-1, keepdims=True) + EPSILON)


def norm_back(upstream, normed, gain_vec, factor):
    scaled = upstream * gain_vec
    return factor * (scaled - normed * jnp.mean(scaled * normed, axis=-1, keepdims=True))


def swiglu_back(hidden_back, gate_proj, up_proj):
    sigmoid_gate = jax.nn.sigmoid(gate_proj)
    gate_back = hidden_back * up_proj * sigmoid_gate * (1.0 + gate_proj * (1.0 - sigmoid_gate))
    up_back = hidden_back * jax.nn.silu(gate_proj)
    return (gate_back.astype(jnp.bfloat16), up_back.astype(jnp.bfloat16))


SMALL = pl.CostEstimate(flops=1024, bytes_accessed=1024, transcendentals=0)


def dot_tn(a, b):
    return lax.dot_general(a, b, (((0,), (0,)), ((), ())), preferred_element_type=jnp.float32)


def fitting(tile, extent):
    return math.gcd(tile, extent)


def first(i):
    return (0, 0)


def along(i):
    return (0, i)


def down_rows(i):
    return (i, 0)


def fill(target_ref, piece_refs):
    start = 0
    for piece_ref in piece_refs:
        count = piece_ref.shape[0]
        target_ref[start : start + count, :] = piece_ref[...]
        start += count


def grads_kernel(lefts, rights, *refs):
    out_refs, (left_ref, right_ref) = refs[lefts + rights : -2], refs[-2:]

    @pl.when(pl.program_id(0) == 0)
    def _():
        fill(left_ref, refs[:lefts])

    fill(right_ref, refs[lefts : lefts + rights])
    total = dot_tn(left_ref[...], right_ref[...])
    start = 0
    for out_ref in out_refs:
        rows = out_ref.shape[0]
        out_ref[...] = total[start : start + rows].astype(jnp.bfloat16)
        start += rows


def weight_grads(lefts, rights, cuts, place=0):
    count = sum(piece.shape[0] for piece in lefts)
    wide = sum(cuts)
    width = rights[0].shape[1]
    tile = fitting(512, width)
    return pl.pallas_call(
        functools.partial(grads_kernel, len(lefts), len(rights)),
        grid=(width // tile,),
        in_specs=[pl.BlockSpec((piece.shape[0], wide), lambda i: (0, place)) for piece in lefts]
        + [pl.BlockSpec((piece.shape[0], tile), along) for piece in rights],
        out_specs=[pl.BlockSpec((rows, tile), along) for rows in cuts],
        out_shape=[jax.ShapeDtypeStruct((rows, width), jnp.bfloat16) for rows in cuts],
        scratch_shapes=[
            pltpu.VMEM((count, wide), jnp.bfloat16),
            pltpu.VMEM((count, tile), jnp.bfloat16),
        ],
        compiler_params=pltpu.CompilerParams(vmem_limit_bytes=VMEM_LIMIT),
        cost_estimate=SMALL,
        name="weight_grads",
    )(*lefts, *rights)


def heads_kernel(upper_ref, right_ref, weight_ref, *refs):
    *piece_refs, keep_ref, give_ref, gain_ref, left_ref = refs
    fill(left_ref, piece_refs)
    total = dot_tn(left_ref[...], right_ref[...])
    count, half, width = keep_ref.shape
    sums = jnp.sum(total * weight_ref[...].astype(jnp.float32), axis=1, keepdims=True)
    gain_ref[...] = jnp.broadcast_to(sums, (total.shape[0], 128)).T[:1]
    blocks = total.astype(jnp.bfloat16).reshape(count, 2, half, width)
    upper = upper_ref[0] == 1
    keep_ref[...] = jnp.where(upper, blocks[:, 1], blocks[:, 0])
    give_ref[...] = jnp.where(upper, blocks[:, 0], blocks[:, 1])


def heads_grads(lefts, right, weight, upper, rows):
    count, width = right.shape
    wide = weight.shape[0]
    tile = fitting(512, wide)
    half = ((tile // rows, rows // 2, width), lambda i: (i, 0, 0))
    whole = ((wide // rows, rows // 2, width), jnp.bfloat16)
    return pl.pallas_call(
        heads_kernel,
        grid=(wide // tile,),
        in_specs=[
            pl.BlockSpec(memory_space=pltpu.SMEM),
            pl.BlockSpec((count, width), first),
            pl.BlockSpec((tile, width), down_rows),
        ]
        + [pl.BlockSpec((piece.shape[0], tile), along) for piece in lefts],
        out_specs=[pl.BlockSpec(*half), pl.BlockSpec(*half), pl.BlockSpec((1, tile), along)],
        out_shape=[
            jax.ShapeDtypeStruct(*whole),
            jax.ShapeDtypeStruct(*whole),
            jax.ShapeDtypeStruct((1, wide), jnp.float32),
        ],
        scratch_shapes=[pltpu.VMEM((count, tile), jnp.bfloat16)],
        compiler_params=pltpu.CompilerParams(vmem_limit_bytes=VMEM_LIMIT),
        cost_estimate=SMALL,
        name="heads_grads",
    )(upper, right, weight, *lefts)


def assemble_kernel(side_ref, *refs):
    out_refs = refs[-3:]
    given = (len(refs) - 3) // 2
    size, part, width = refs[0].shape
    columns = width // 3
    upper = side_ref[0] == 1
    for index, (near_ref, far_ref) in enumerate(zip(refs[:given], refs[given:-3])):
        low = jnp.where(upper, far_ref[...], near_ref[...]).astype(jnp.float32)
        high = jnp.where(upper, near_ref[...], far_ref[...]).astype(jnp.float32)
        for piece, out_ref in enumerate(out_refs):
            for source in range(size):
                place = slice(source * columns, (source + 1) * columns)
                taken = slice(piece * columns, (piece + 1) * columns)
                for start, block in ((index, low), (given + index, high)):
                    out_ref[start * part : (start + 1) * part, place] = block[source, :, taken]


def assemble(near, far, side):
    size, part, width = near[0].shape
    shape = (2 * len(near) * part, size * width // 3)
    vmem = pl.BlockSpec(memory_space=pltpu.VMEM)
    return pl.pallas_call(
        assemble_kernel,
        in_specs=[pl.BlockSpec(memory_space=pltpu.SMEM)] + [vmem] * (2 * len(near)),
        out_specs=[vmem] * 3,
        out_shape=[jax.ShapeDtypeStruct(shape, jnp.float32)] * 3,
        compiler_params=pltpu.CompilerParams(vmem_limit_bytes=VMEM_LIMIT),
        cost_estimate=SMALL,
        name="assemble",
    )(side, *near, *far)


def sums_kernel(*refs):
    out_ref = refs[-1]
    count = (len(refs) - 1) // 2
    start = 0
    for part_ref, other_ref in zip(refs[:count], refs[count:-1]):
        rows = part_ref.shape[0]
        out_ref[start : start + rows, :] = part_ref[...].astype(jnp.float32) + other_ref[
            ...
        ].astype(jnp.float32)
        start += rows


def sum_pieces(parts, others):
    width = parts[0].shape[1]
    tile = fitting(512, width)
    total = sum(piece.shape[0] for piece in parts)
    return pl.pallas_call(
        sums_kernel,
        grid=(width // tile,),
        in_specs=[pl.BlockSpec((piece.shape[0], tile), along) for piece in (*parts, *others)],
        out_specs=[pl.BlockSpec((total, tile), along)],
        out_shape=[jax.ShapeDtypeStruct((total, width), jnp.float32)],
        compiler_params=pltpu.CompilerParams(vmem_limit_bytes=VMEM_LIMIT),
        cost_estimate=SMALL,
        name="sum_pieces",
    )(*parts, *others)


class Ring:
    def __init__(self, size):
        self.size = size
        self.pairs = size // 2
        self.reach = self.pairs // 2
        columns = self.pairs // 2
        self.order = [2 * a for a in range(columns)] + [2 * a + 1 for a in reversed(range(columns))]
        self.ahead = []
        self.behind = []
        for place, pair in enumerate(self.order):
            following = self.order[(place + 1) % self.pairs]
            for lane in range(2):
                self.ahead.append((2 * pair + lane, 2 * following + lane))
                self.behind.append((2 * following + lane, 2 * pair + lane))
        self.across = [(device, device ^ 1) for device in range(size)]

    def slots(self):
        offsets = [(0, 0), (0, 1)]
        for step in range(1, self.reach):
            offsets += [(-step, 0), (step, 0), (-step, 1), (step, 1)]
        offsets += [(self.reach, 0), (self.reach, 1)]
        table = np.zeros((self.size, self.size), np.int32)
        for device in range(self.size):
            place = self.order.index(device // 2)
            for slot, (offset, flip) in enumerate(offsets):
                pair = self.order[(place + offset) % self.pairs]
                table[device, 2 * pair + (device % 2 ^ flip)] = slot
        return table

    def forward(self, array):
        return lax.ppermute(array, "wide", self.ahead)

    def backward(self, array):
        return lax.ppermute(array, "wide", self.behind)

    def twin(self, array):
        return lax.ppermute(array, "wide", self.across)

    def gather(self, rows, groups):
        groups.append([rows, self.twin(rows)])
        ahead = behind = rows
        middle = rows.shape[0] // 2
        for step in range(1, self.reach + 1):
            if step == self.reach:
                ahead, behind = ahead[:middle], behind[middle:]
            (ahead, behind), _ = yield ((self.forward, ahead), (self.backward, behind)), ()
            groups.append([ahead, behind, self.twin(ahead), self.twin(behind)])

    def scatter(self, make):
        def pair_sum(step, *held):
            mine, other = make(step, *held)
            return mine + self.twin(other.astype(jnp.bfloat16)).astype(jnp.float32)

        total = pair_sum(self.reach)
        middle = total.shape[0] // 2
        low, high = total[:middle], total[middle:]
        for step in range(self.reach - 1, -1, -1):
            held = (low.astype(jnp.bfloat16), high.astype(jnp.bfloat16))
            (down, up), (total,) = (
                yield (
                    ((self.backward, held[0]), (self.forward, held[1])),
                    (pair_sum(step, *held),),
                )
            )
            down, up = down.astype(jnp.float32), up.astype(jnp.float32)
            if step == 0:
                return total + down + up
            count = total.shape[0] // 2
            low, high = total[:count], total[count:]
            if step == self.reach - 1:
                low = jnp.concatenate([low[:middle] + down, low[middle:]], axis=0)
                high = jnp.concatenate([high[:middle], high[middle:] + up], axis=0)
            else:
                low, high = low + down, high + up

    def total(self, array):
        def flip(bit):
            pairs = [(i, i ^ bit) for i in range(self.size)]
            return functools.partial(lax.ppermute, axis_name="wide", perm=pairs)

        ways = [swapped]
        bit = 4
        while bit < self.size:
            ways.insert(0 if bit > 4 else 1, flip(bit))
            bit *= 2
        for way in ways:
            ((other,), _) = yield ((way, array),), ()
            array = array + other
        for bit in (2, 1):
            array = array + flip(bit)(array)
        return array


class Stream:
    def __init__(self, hops):
        self.hops = hops
        self.asked, self.beside = next(hops)
        self.result = None

    def post(self):
        return [send(array) for send, array in self.asked]

    def land(self, arrived, beside):
        try:
            self.asked, self.beside = self.hops.send((arrived, beside))
        except StopIteration as end:
            self.asked, self.beside = None, ()
            self.result = end.value


class Swaps:
    def __init__(self):
        self.waiting = []
        self.done = {}
        self.parts = {}

    def add(self, name, parts):
        self.parts[name] = list(parts)
        self.done[name] = []
        self.waiting += [(name, index) for index in range(len(parts))]

    def sums(self, name):
        return (self.parts[name], self.done[name])


def joined(*lists):
    held = list(lax.optimization_barrier(tuple(array for part in lists for array in part)))
    result = []
    for part in lists:
        result.append(held[: len(part)])
        held = held[len(part) :]
    return result


def hop(streams, swaps=None, count=1, beside=(), work=None, given=()):
    streams = [stream for stream in streams if stream.asked is not None]
    ready = []
    if swaps is not None:
        ready, swaps.waiting = swaps.waiting[:count], swaps.waiting[count:]
    asked = [array for stream in streams for _, array in stream.asked]
    if work is not None:
        flat, tree = jax.tree.flatten(given)
        beside = work(*jax.tree.unflatten(tree, joined(asked, flat)[1]))
    pieces = joined(asked, [swaps.parts[name][index] for name, index in ready])[1]
    lists = [stream.post() for stream in streams]
    lists += [stream.beside for stream in streams]
    lists.append([swapped(piece) for piece in pieces])
    lists.append(beside)
    *lists, moved, beside = joined(*lists)
    for (name, _), piece in zip(ready, moved):
        swaps.done[name].append(piece)
    for place, stream in enumerate(streams):
        stream.land(lists[place], lists[len(streams) + place])
    return beside


def travel(stream, swaps=None, count=1):
    while stream.asked is not None:
        hop([stream], swaps, count)
    return stream.result


def swapped(part):
    return lax.ppermute(part, "narrow", [(0, 1), (1, 0)])


def after(array, *others):
    return lax.optimization_barrier((array,) + others)[0]


def halves(array):
    middle = array.shape[0] // 2
    return array[:middle], array[middle:]


def shards(
    ring,
    layer_input,
    lengths,
    attn_gain,
    w_query,
    w_key,
    w_value,
    w_out,
    mlp_gain,
    w_gate,
    w_up,
    w_down,
    cotangent,
):
    size = ring.size
    local_rows = layer_input.shape[1]
    model_width = layer_input.shape[2]
    row_count = local_rows * size
    own_width = model_width // size
    width = max(own_width, 2 * HEAD_DIM)
    sharing = width // own_width
    device = lax.axis_index("wide")
    member = device % sharing
    slot_of = lax.dynamic_index_in_dim(jnp.asarray(ring.slots()), device, keepdims=False)

    def own_columns(array):
        if sharing == 1:
            return array
        runs = array.reshape(array.shape[0], -1, sharing, own_width)
        return lax.dynamic_index_in_dim(runs, member, axis=2, keepdims=False).reshape(
            array.shape[0], -1
        )

    positions = device * local_rows + jnp.arange(local_rows, dtype=jnp.int32)
    valid_rows = (positions < lengths[0]).astype(jnp.float32)[:, None]
    cosine, sine = rotary_tables(row_count, width)
    inputs = layer_input[0].astype(jnp.float32)
    gain_one = attn_gain.astype(jnp.float32)
    gain_two = mlp_gain.astype(jnp.float32)
    y_back = cotangent[0].astype(jnp.float32) * valid_rows
    mlp_back = y_back.astype(jnp.bfloat16)

    blocks = jnp.concatenate(
        [w.reshape(own_width, -1, width) for w in (w_query, w_key, w_value)], axis=-1
    ).transpose(1, 0, 2)
    blocks = jnp.repeat(blocks, sharing, axis=0)
    half_rows = own_width // 2
    upper = lax.axis_index("narrow") == 1
    w_out_heads = w_out
    if sharing > 1:
        near = [list(range(a, a + sharing)) for a in range(0, size, sharing)]
        w_out_heads = lax.all_gather(w_out, "wide", axis=0, tiled=True, axis_index_groups=near)
    units = w_gate.shape[0]
    w_both = jnp.concatenate([w_gate, w_up], axis=0)
    factor_one = rms_factor(inputs)
    normed_one = inputs * factor_one
    norm_one = (normed_one * gain_one).astype(jnp.bfloat16)
    sent = jnp.where(upper, blocks[:, half_rows:], blocks[:, :half_rows])
    near_half = lax.all_to_all(after(sent, norm_one), "wide", 0, 0, tiled=True)
    group_one = []
    one = Stream(ring.gather(norm_one, group_one))
    hop([one])
    cosine, sine = hop([one], beside=(cosine, sine))
    while one.asked is not None:
        hop([one])
    far_half = swapped(near_half)
    w_heads = jnp.stack(
        [jnp.where(upper, far_half, near_half), jnp.where(upper, near_half, far_half)], axis=1
    ).reshape(model_width, 3 * width)
    pieces_one = sum(group_one, [])
    lin = dot_nn(jnp.concatenate(pieces_one, axis=0), w_heads)
    starts = [0]
    for rows in group_one:
        starts.append(starts[-1] + sum(piece.shape[0] for piece in rows))

    def group_of(array, step):
        return array[starts[step] : starts[step + 1]]

    group_back = []
    back = Stream(ring.gather(after(mlp_back, lin), group_back))
    heads_attention, query, key, value, logs = hop(
        [back], beside=attention_forward(slot_of, lengths, lin, cosine, sine)
    )
    attention = own_columns(heads_attention)

    def residual_part(step, *held):
        mine, other = halves(group_of(attention, step))
        return dot_nn(mine, w_out), dot_nn(other, w_out)

    mixed = Stream(ring.scatter(residual_part))
    while mixed.asked is not None:
        hop([mixed, back])
    residual = inputs + mixed.result
    factor_two = rms_factor(residual)
    normed_two = residual * factor_two
    norm_two = (normed_two * gain_two).astype(jnp.bfloat16)
    group_two = []
    two = Stream(ring.gather(norm_two, group_two))
    hidden = []
    both_back = []

    def feed(step):
        both = dot_nt(jnp.concatenate(group_two[step], axis=0), w_both)
        gate_proj, up_proj = both[:, :units], both[:, units:]
        hidden_back = dot_nt(jnp.concatenate(group_back[step], axis=0), w_down)
        return (
            (jax.nn.silu(gate_proj) * up_proj).astype(jnp.bfloat16),
            jnp.concatenate(swiglu_back(hidden_back, gate_proj, up_proj), axis=1),
        )

    for step in range(ring.reach):
        fed = hop([two], beside=feed(step))
        hidden.append(fed[0])
        both_back.append(fed[1])
    fed = feed(ring.reach)
    hidden.append(fed[0])
    both_back.append(fed[1])

    def pull_part(step, *held):
        mine, other = halves(after(both_back[step], *held))
        return dot_nn(mine, w_both), dot_nn(other, w_both)

    def mlp_part(step, *held):
        mine, other = halves(after(hidden[step], *(held or (branch_back,))))
        return dot_nn(mine, w_down), dot_nn(other, w_down)

    swaps = Swaps()
    cuts = [[units // 16 * count for count in row] for row in ((4, 4, 8), (8, 8), (2, 8, 6))]
    pull = Stream(ring.scatter(pull_part))
    hop([pull])
    swaps.add(
        "down",
        hop(
            [pull],
            work=functools.partial(weight_grads, cuts=cuts[0]),
            given=(hidden, sum(group_back, [])),
        ),
    )
    norm_two_back = travel(pull, swaps)
    residual_back = y_back + norm_back(norm_two_back, normed_two, gain_two, factor_two)
    gain_two_term = jnp.sum(norm_two_back * normed_two, axis=0)
    branch_back = residual_back.astype(jnp.bfloat16)
    mlp = Stream(ring.scatter(mlp_part))
    group_branch = []
    branch = Stream(ring.gather(branch_back, group_branch))
    pieces_two = sum(group_two, [])
    for place, name in enumerate(("gate", "up")):
        parts = hop(
            [branch, mlp],
            swaps,
            work=functools.partial(
                weight_grads, cuts=cuts[1 + place], place=place
            ),
            given=(both_back, pieces_two),
        )
        swaps.add(name, parts)
    (down_sum,) = hop([branch, mlp], swaps, work=sum_pieces, given=swaps.sums("down"))
    while branch.asked is not None:
        hop([branch], swaps)
    upstream = jnp.concatenate(
        [
            dot_nt(jnp.concatenate(rows, axis=0), w_out_heads).astype(jnp.bfloat16)
            for rows in group_branch
        ],
        axis=0,
    )
    (lin_back,) = hop(
        [mlp],
        swaps,
        beside=attention_backward(
            slot_of, lengths, query, key, value, heads_attention, upstream, logs, cosine, sine
        ),
    )
    lin_back = own_columns(lin_back)
    w_own = own_columns(w_heads)

    def input_part(step, *held):
        mine, other = halves(after(group_of(lin_back, step), *held))
        return dot_nt(mine, w_own), dot_nt(other, w_own)

    pulled = Stream(ring.scatter(input_part))
    side = lax.axis_index("narrow").reshape(1)
    keep, give, gain_one_sum = hop(
        [pulled],
        swaps,
        work=functools.partial(heads_grads, rows=own_width),
        given=(pieces_one, lin_back, w_own, side),
    )
    while mlp.asked is not None:
        hop([mlp])
    totals = Stream(ring.total(jnp.stack([gain_one_sum[0] / gain_one, gain_two_term])))

    def before(piece, left, rights, parts, others):
        return (
            swapped(piece),
            *weight_grads([left], rights, (own_width,)),
            *sum_pieces(parts, others),
        )

    given, out_part, gate_sum = hop(
        [pulled, totals],
        work=before,
        given=(give, attention, sum(group_branch, []), *swaps.sums("gate")),
    )
    heads_sum = lax.all_to_all(
        (keep.astype(jnp.float32) + given.astype(jnp.float32)).astype(jnp.bfloat16),
        "wide",
        0,
        0,
        tiled=True,
    )
    swaps.add("out", [out_part])
    hop([pulled, totals], swaps)
    (up_sum,) = hop([pulled, totals], work=sum_pieces, given=swaps.sums("up"))
    while pulled.asked is not None or totals.asked is not None:
        hop([pulled, totals])
    norm_one_back = pulled.result
    block_output = (residual + after(mlp.result, norm_one_back)).astype(jnp.bfloat16)
    gain_totals = totals.result
    far = swapped(heads_sum)
    (out_sum,) = sum_pieces(*swaps.sums("out"))
    attention_sums = assemble([heads_sum], [far], side)
    input_back = residual_back + norm_back(norm_one_back, normed_one, gain_one, factor_one)
    return (
        block_output[None],
        input_back[None],
        gain_totals[0],
        attention_sums[0],
        attention_sums[1],
        attention_sums[2],
        out_sum,
        gain_totals[1],
        gate_sum,
        up_sum,
        down_sum,
    )


def solution(mesh):
    placed = (
        P("narrow", "wide", None),
        P("narrow"),
        P(),
        P("wide", None),
        P("wide", None),
        P("wide", None),
        P("wide", None),
        P(),
        P("wide", None),
        P("wide", None),
        P("wide", None),
        P("narrow", "wide", None),
    )
    return jax.shard_map(
        functools.partial(shards, Ring(mesh.shape["wide"])),
        mesh=mesh,
        in_specs=placed,
        out_specs=(
            P("narrow", "wide", None),
            P("narrow", "wide", None),
            P(),
            P("wide", None),
            P("wide", None),
            P("wide", None),
            P("wide", None),
            P(),
            P("wide", None),
            P("wide", None),
            P("wide", None),
        ),
        check_vma=False,
    )
```

```python
import functools
import jax
import jax.numpy as jnp
from jax import lax
from jax.experimental import pallas as pl
from jax.experimental.pallas import tpu as pltpu
import math
import numpy as np
from jax.sharding import PartitionSpec as P

HEAD_DIM = 64
NEGATIVE = -1e30
VMEM_LIMIT = 56 * 1024 * 1024


def dot_nt(a, b):
    return lax.dot_general(a, b, (((1,), (1,)), ((), ())), preferred_element_type=jnp.float32)


def dot_nn(a, b):
    return lax.dot_general(a, b, (((1,), (0,)), ((), ())), preferred_element_type=jnp.float32)


def half_turn(tensor):
    width = tensor.shape[-1]
    half_dim = HEAD_DIM // 2
    lane = lax.broadcasted_iota(jnp.int32, tensor.shape, 1)
    return jnp.where(
        lane % HEAD_DIM < half_dim,
        -pltpu.roll(tensor, width - half_dim, 1),
        pltpu.roll(tensor, half_dim, 1),
    )


def head_lanes(block, head):
    lane = lax.broadcasted_iota(jnp.int32, block.shape, 1)
    return jnp.where(lane // HEAD_DIM == head, block, jnp.zeros_like(block))


def forward_kernel(
    slot_ref, length_ref, lin_ref, cos_ref, sin_ref,
    att_ref, query_ref, key_ref, value_ref, log_ref,
    turned, attn_nat,
):
    rows = query_ref.shape[0]
    width = query_ref.shape[1]
    heads = width // HEAD_DIM
    slots = slot_ref.shape[0]
    shard = rows // slots
    length = length_ref[0]
    scale = HEAD_DIM ** (-0.5)

    @pl.loop(0, slots, unroll=4)
    def _(place):
        source = pl.ds(pl.multiple_of(slot_ref[place] * shard, shard), shard)
        target = pl.ds(pl.multiple_of(place * shard, shard), shard)
        cosine = cos_ref[target, :]
        sine = sin_ref[target, :]
        query_lin = lin_ref[source, 0:width]
        key_lin = lin_ref[source, width : 2 * width]
        value_lin = lin_ref[source, 2 * width : 3 * width]
        query = (query_lin * cosine + half_turn(query_lin) * sine).astype(jnp.bfloat16)
        query_ref[target, :] = (query.astype(jnp.float32) * scale).astype(jnp.bfloat16)
        key_ref[target, :] = (key_lin * cosine + half_turn(key_lin) * sine).astype(jnp.bfloat16)
        value_ref[target, :] = value_lin.astype(jnp.bfloat16)
        turned[:, target] = value_lin.T.astype(jnp.bfloat16)

    block_q = min(1024, rows)
    block_k = min(512, rows)

    @pl.loop(0, rows // block_q)
    def _(i):
        q_first = pl.multiple_of(i * block_q, block_q)
        query = query_ref[pl.ds(q_first, block_q), :]
        parts = [head_lanes(query, h) for h in range(heads)]
        q_pos = q_first + lax.broadcasted_iota(jnp.int32, (1, block_q), 1)
        limit = jnp.minimum(q_pos, length - 1)
        full = jnp.minimum(q_first, length) // block_k
        stop = (jnp.minimum(q_first + block_q, length) + block_k - 1) // block_k

        def step(j, state, masked):
            k_first = pl.multiple_of(j * block_k, block_k)
            key = key_ref[pl.ds(k_first, block_k), :]
            out = []
            if masked:
                k_pos = k_first + lax.broadcasted_iota(jnp.int32, (block_k, block_q), 0)
                allowed = k_pos <= limit
            for h in range(heads):
                best, total, acc = state[3 * h : 3 * h + 3]
                scores = dot_nt(key, parts[h])
                if masked:
                    scores = jnp.where(allowed, scores, NEGATIVE)
                new_best = jnp.maximum(best, jnp.max(scores, axis=0, keepdims=True))
                weight = jnp.exp(scores - new_best)
                shrink = jnp.exp(best - new_best)
                total = total * shrink + jnp.sum(weight, axis=0, keepdims=True)
                value_t = turned[h * HEAD_DIM : (h + 1) * HEAD_DIM, pl.ds(k_first, block_k)]
                acc = acc * shrink + dot_nn(value_t, weight.astype(jnp.bfloat16))
                out += [new_best, total, acc]
            return tuple(out)

        state = ()
        for h in range(heads):
            state += (
                jnp.full((1, block_q), NEGATIVE, jnp.float32),
                jnp.zeros((1, block_q), jnp.float32),
                jnp.zeros((HEAD_DIM, block_q), jnp.float32),
            )
        state = lax.fori_loop(0, full, functools.partial(step, masked=False), state)
        state = lax.fori_loop(full, stop, functools.partial(step, masked=True), state)
        for h in range(heads):
            best, total, acc = state[3 * h : 3 * h + 3]
            log_ref[h : h + 1, pl.ds(q_first, block_q)] = best + jnp.log(total)
        joined = jnp.concatenate([state[3 * h + 2] / state[3 * h + 1] for h in range(heads)], axis=0)
        attn_nat[pl.ds(q_first, block_q), :] = joined.T.astype(jnp.bfloat16)

    @pl.loop(0, slots, unroll=4)
    def _(place):
        source = pl.ds(pl.multiple_of(slot_ref[place] * shard, shard), shard)
        target = pl.ds(pl.multiple_of(place * shard, shard), shard)
        att_ref[source, :] = attn_nat[target, :]


def attention_forward(slot_of, length, lin, cosine, sine):
    rows, width = cosine.shape
    vmem = pl.BlockSpec(memory_space=pltpu.VMEM)
    smem = pl.BlockSpec(memory_space=pltpu.SMEM)
    half = jax.ShapeDtypeStruct((rows, width), jnp.bfloat16)
    return pl.pallas_call(
        forward_kernel,
        out_shape=(half, half, half, half, jax.ShapeDtypeStruct((8, rows), jnp.float32)),
        in_specs=[smem, smem, vmem, vmem, vmem],
        out_specs=(vmem,) * 5,
        scratch_shapes=[
            pltpu.VMEM((width, rows), jnp.bfloat16),
            pltpu.VMEM((rows, width), jnp.bfloat16),
        ],
        compiler_params=pltpu.CompilerParams(vmem_limit_bytes=VMEM_LIMIT),
        cost_estimate=pl.CostEstimate(
            flops=4 * rows * rows * width, bytes_accessed=24 * rows * width, transcendentals=rows * rows
        ),
        name="attention_forward",
    )(slot_of, length, lin, cosine, sine)


def backward_kernel(
    slot_ref, length_ref, query_ref, key_ref, value_ref, att_ref, up_ref, log_ref, cos_ref, sin_ref,
    *refs,
):
    *out_refs, out_ref, key_t, up_nat, delta, key_acc, value_acc, query_acc = refs
    rows = query_ref.shape[0]
    width = query_ref.shape[1]
    heads = width // HEAD_DIM
    slots = slot_ref.shape[0]
    shard = rows // slots
    length = length_ref[0]
    scale = HEAD_DIM ** (-0.5)
    key_acc[...] = jnp.zeros_like(key_acc)
    value_acc[...] = jnp.zeros_like(value_acc)

    @pl.loop(0, slots, unroll=4)
    def _(place):
        source = pl.ds(pl.multiple_of(slot_ref[place] * shard, shard), shard)
        target = pl.ds(pl.multiple_of(place * shard, shard), shard)
        upstream = up_ref[source, :]
        up_nat[target, :] = upstream
        product = (upstream.astype(jnp.float32) * att_ref[source, :].astype(jnp.float32)).T
        for h in range(heads):
            delta[h : h + 1, target] = jnp.sum(
                product[h * HEAD_DIM : (h + 1) * HEAD_DIM, :], axis=0, keepdims=True
            )
        key_t[:, target] = key_ref[target, :].astype(jnp.float32).T.astype(jnp.bfloat16)

    block_q = min(512, rows)
    block_k = min(512, rows)

    @pl.loop(0, rows // block_q)
    def _(i):
        q_first = pl.multiple_of(i * block_q, block_q)
        here = pl.ds(q_first, block_q)
        query = query_ref[here, :]
        upstream = up_nat[here, :]
        q_parts = [head_lanes(query, h) for h in range(heads)]
        u_parts = [head_lanes(upstream, h) for h in range(heads)]
        logs = [log_ref[h : h + 1, here] for h in range(heads)]
        deltas = [delta[h : h + 1, here] for h in range(heads)]
        q_pos = q_first + lax.broadcasted_iota(jnp.int32, (1, block_q), 1)
        limit = jnp.minimum(q_pos, length - 1)
        full = jnp.minimum(q_first, length) // block_k
        stop = (jnp.minimum(q_first + block_q, length) + block_k - 1) // block_k

        def step(j, state, masked):
            k_first = pl.multiple_of(j * block_k, block_k)
            there = pl.ds(k_first, block_k)
            key = key_ref[there, :]
            value = value_ref[there, :]
            if masked:
                k_pos = k_first + lax.broadcasted_iota(jnp.int32, (block_k, block_q), 0)
                allowed = k_pos <= limit
            out = []
            key_add = None
            for h in range(heads):
                prob = jnp.exp(dot_nt(key, q_parts[h]) - logs[h])
                if masked:
                    prob = jnp.where(allowed, prob, 0.0)
                pulled = dot_nt(value, u_parts[h])
                score_back = (prob * (pulled - deltas[h])).astype(jnp.bfloat16)
                one = dot_nn(prob.astype(jnp.bfloat16), u_parts[h])
                two = dot_nn(score_back, q_parts[h])
                value_add = one if key_add is None else value_add + one
                key_add = two if key_add is None else key_add + two
                out.append(
                    state[h] + dot_nn(key_t[h * HEAD_DIM : (h + 1) * HEAD_DIM, there], score_back)
                )
            value_acc[there, :] += value_add
            key_acc[there, :] += key_add
            return tuple(out)

        state = tuple(jnp.zeros((HEAD_DIM, block_q), jnp.float32) for h in range(heads))
        state = lax.fori_loop(0, full, functools.partial(step, masked=False), state)
        state = lax.fori_loop(full, stop, functools.partial(step, masked=True), state)
        query_acc[here, :] = (jnp.concatenate(state, axis=0) * scale).T

    @pl.loop(0, slots, unroll=4)
    def _(place):
        source = pl.ds(pl.multiple_of(slot_ref[place] * shard, shard), shard)
        target = pl.ds(pl.multiple_of(place * shard, shard), shard)
        cosine = cos_ref[target, :]
        sine = sin_ref[target, :]
        for piece, held in enumerate((query_acc, key_acc)):
            grad = held[target, :]
            out_ref[source, piece * width : (piece + 1) * width] = (
                grad * cosine - half_turn(grad * sine)
            ).astype(jnp.bfloat16)
        out_ref[source, 2 * width : 3 * width] = value_acc[target, :].astype(jnp.bfloat16)

    start = 0
    for group_ref in out_refs:
        count = group_ref.shape[0]
        group_ref[...] = out_ref[start : start + count, :]
        start += count


def attention_backward(
    slot_of, length, query, key, value, att, upstream, logs, cosine, sine, group_rows
):
    rows, width = query.shape
    vmem = pl.BlockSpec(memory_space=pltpu.VMEM)
    smem = pl.BlockSpec(memory_space=pltpu.SMEM)
    return pl.pallas_call(
        backward_kernel,
        out_shape=[
            jax.ShapeDtypeStruct((count, 3 * width), jnp.bfloat16) for count in group_rows
        ],
        in_specs=[smem, smem] + [vmem] * 8,
        out_specs=[vmem] * len(group_rows),
        scratch_shapes=[
            pltpu.VMEM((rows, 3 * width), jnp.bfloat16),
            pltpu.VMEM((width, rows), jnp.bfloat16),
            pltpu.VMEM((rows, width), jnp.bfloat16),
            pltpu.VMEM((8, rows), jnp.float32),
            pltpu.VMEM((rows, width), jnp.float32),
            pltpu.VMEM((rows, width), jnp.float32),
            pltpu.VMEM((rows, width), jnp.float32),
        ],
        compiler_params=pltpu.CompilerParams(vmem_limit_bytes=VMEM_LIMIT),
        cost_estimate=pl.CostEstimate(
            flops=10 * rows * rows * width, bytes_accessed=36 * rows * width, transcendentals=rows * rows
        ),
        name="attention_backward",
    )(slot_of, length, query, key, value, att, upstream, logs, cosine, sine)


EPSILON = 1e-05
THETA = 130000.0


def contract_rows(left_side, right_side):
    return lax.dot_general(
        left_side, right_side, (((0,), (0,)), ((), ())), preferred_element_type=jnp.float32
    )


def rotary_tables(row_count, width):
    half_dim = HEAD_DIM // 2
    feature = (jnp.arange(width, dtype=jnp.int32) % half_dim).astype(jnp.float32)
    frequency = THETA ** (-feature * 2.0 / HEAD_DIM)
    angles = jnp.arange(row_count, dtype=jnp.float32)[:, None] * frequency[None, :]
    return (jnp.cos(angles), jnp.sin(angles))


def rms_factor(matrix):
    return lax.rsqrt(jnp.mean(matrix * matrix, axis=-1, keepdims=True) + EPSILON)


def norm_back(upstream, normed, gain_vec, factor):
    scaled = upstream * gain_vec
    return factor * (scaled - normed * jnp.mean(scaled * normed, axis=-1, keepdims=True))


def swiglu_back(hidden_back, gate_proj, up_proj):
    sigmoid_gate = jax.nn.sigmoid(gate_proj)
    gate_back = hidden_back * up_proj * sigmoid_gate * (1.0 + gate_proj * (1.0 - sigmoid_gate))
    up_back = hidden_back * jax.nn.silu(gate_proj)
    return (gate_back.astype(jnp.bfloat16), up_back.astype(jnp.bfloat16))


SMALL = pl.CostEstimate(flops=1024, bytes_accessed=1024, transcendentals=0)


def dot_tn(a, b):
    return lax.dot_general(a, b, (((0,), (0,)), ((), ())), preferred_element_type=jnp.float32)


def fitting(tile, extent):
    return math.gcd(tile, extent)


def first(i):
    return (0, 0)


def along(i):
    return (0, i)


def down_rows(i):
    return (i, 0)


def fill(target_ref, piece_refs):
    start = 0
    for piece_ref in piece_refs:
        count = piece_ref.shape[0]
        target_ref[start : start + count, :] = piece_ref[...]
        start += count


def grads_kernel(lefts, rights, *refs):
    out_refs, (left_ref, right_ref) = refs[lefts + rights : -2], refs[-2:]

    @pl.when(pl.program_id(0) == 0)
    def _():
        fill(left_ref, refs[:lefts])

    fill(right_ref, refs[lefts : lefts + rights])
    total = dot_tn(left_ref[...], right_ref[...])
    start = 0
    for out_ref in out_refs:
        rows = out_ref.shape[0]
        out_ref[...] = total[start : start + rows].astype(jnp.bfloat16)
        start += rows


def weight_grads(lefts, rights, cuts, place=0):
    count = sum(piece.shape[0] for piece in lefts)
    wide = sum(cuts)
    width = rights[0].shape[1]
    tile = fitting(512, width)
    return pl.pallas_call(
        functools.partial(grads_kernel, len(lefts), len(rights)),
        grid=(width // tile,),
        in_specs=[pl.BlockSpec((piece.shape[0], wide), lambda i: (0, place)) for piece in lefts]
        + [pl.BlockSpec((piece.shape[0], tile), along) for piece in rights],
        out_specs=[pl.BlockSpec((rows, tile), along) for rows in cuts],
        out_shape=[jax.ShapeDtypeStruct((rows, width), jnp.bfloat16) for rows in cuts],
        scratch_shapes=[
            pltpu.VMEM((count, wide), jnp.bfloat16),
            pltpu.VMEM((count, tile), jnp.bfloat16),
        ],
        compiler_params=pltpu.CompilerParams(vmem_limit_bytes=VMEM_LIMIT),
        cost_estimate=SMALL,
        name="weight_grads",
    )(*lefts, *rights)


def heads_kernel(rights, upper_ref, weight_ref, *refs):
    *piece_refs, keep_ref, give_ref, gain_ref, left_ref, right_ref = refs

    @pl.when(pl.program_id(0) == 0)
    def _():
        fill(right_ref, piece_refs[:rights])

    fill(left_ref, piece_refs[rights:])
    total = dot_tn(left_ref[...], right_ref[...])
    count, half, width = keep_ref.shape
    sums = jnp.sum(total * weight_ref[...].astype(jnp.float32), axis=1, keepdims=True)
    gain_ref[...] = jnp.broadcast_to(sums, (total.shape[0], 128)).T[:1]
    blocks = total.astype(jnp.bfloat16).reshape(count, 2, half, width)
    upper = upper_ref[0] == 1
    keep_ref[...] = jnp.where(upper, blocks[:, 1], blocks[:, 0])
    give_ref[...] = jnp.where(upper, blocks[:, 0], blocks[:, 1])


def heads_grads(lefts, rights, weight, upper, rows):
    count = sum(piece.shape[0] for piece in rights)
    wide, width = weight.shape
    tile = fitting(512, wide)
    half = ((tile // rows, rows // 2, width), lambda i: (i, 0, 0))
    whole = ((wide // rows, rows // 2, width), jnp.bfloat16)
    return pl.pallas_call(
        functools.partial(heads_kernel, len(rights)),
        grid=(wide // tile,),
        in_specs=[
            pl.BlockSpec(memory_space=pltpu.SMEM),
            pl.BlockSpec((tile, width), down_rows),
        ]
        + [pl.BlockSpec(piece.shape, first) for piece in rights]
        + [pl.BlockSpec((piece.shape[0], tile), along) for piece in lefts],
        out_specs=[pl.BlockSpec(*half), pl.BlockSpec(*half), pl.BlockSpec((1, tile), along)],
        out_shape=[
            jax.ShapeDtypeStruct(*whole),
            jax.ShapeDtypeStruct(*whole),
            jax.ShapeDtypeStruct((1, wide), jnp.float32),
        ],
        scratch_shapes=[
            pltpu.VMEM((count, tile), jnp.bfloat16),
            pltpu.VMEM((count, width), jnp.bfloat16),
        ],
        compiler_params=pltpu.CompilerParams(vmem_limit_bytes=VMEM_LIMIT),
        cost_estimate=SMALL,
        name="heads_grads",
    )(upper, weight, *rights, *lefts)


def assemble_kernel(side_ref, *refs):
    out_refs = refs[-3:]
    given = (len(refs) - 3) // 2
    size, part, width = refs[0].shape
    columns = width // 3
    upper = side_ref[0] == 1
    for index, (near_ref, far_ref) in enumerate(zip(refs[:given], refs[given:-3])):
        low = jnp.where(upper, far_ref[...], near_ref[...]).astype(jnp.float32)
        high = jnp.where(upper, near_ref[...], far_ref[...]).astype(jnp.float32)
        for piece, out_ref in enumerate(out_refs):
            for source in range(size):
                place = slice(source * columns, (source + 1) * columns)
                taken = slice(piece * columns, (piece + 1) * columns)
                for start, block in ((index, low), (given + index, high)):
                    out_ref[start * part : (start + 1) * part, place] = block[source, :, taken]


def assemble(near, far, side):
    size, part, width = near[0].shape
    shape = (2 * len(near) * part, size * width // 3)
    vmem = pl.BlockSpec(memory_space=pltpu.VMEM)
    return pl.pallas_call(
        assemble_kernel,
        in_specs=[pl.BlockSpec(memory_space=pltpu.SMEM)] + [vmem] * (2 * len(near)),
        out_specs=[vmem] * 3,
        out_shape=[jax.ShapeDtypeStruct(shape, jnp.float32)] * 3,
        compiler_params=pltpu.CompilerParams(vmem_limit_bytes=VMEM_LIMIT),
        cost_estimate=SMALL,
        name="assemble",
    )(side, *near, *far)


def sums_kernel(*refs):
    out_ref = refs[-1]
    count = (len(refs) - 1) // 2
    start = 0
    for part_ref, other_ref in zip(refs[:count], refs[count:-1]):
        rows = part_ref.shape[0]
        out_ref[start : start + rows, :] = part_ref[...].astype(jnp.float32) + other_ref[
            ...
        ].astype(jnp.float32)
        start += rows


def sum_pieces(parts, others):
    width = parts[0].shape[1]
    tile = fitting(512, width)
    total = sum(piece.shape[0] for piece in parts)
    return pl.pallas_call(
        sums_kernel,
        grid=(width // tile,),
        in_specs=[pl.BlockSpec((piece.shape[0], tile), along) for piece in (*parts, *others)],
        out_specs=[pl.BlockSpec((total, tile), along)],
        out_shape=[jax.ShapeDtypeStruct((total, width), jnp.float32)],
        compiler_params=pltpu.CompilerParams(vmem_limit_bytes=VMEM_LIMIT),
        cost_estimate=SMALL,
        name="sum_pieces",
    )(*parts, *others)


class Ring:
    def __init__(self, size):
        self.size = size
        self.pairs = size // 2
        self.reach = self.pairs // 2
        columns = self.pairs // 2
        self.order = [2 * a for a in range(columns)] + [2 * a + 1 for a in reversed(range(columns))]
        self.ahead = []
        self.behind = []
        for place, pair in enumerate(self.order):
            following = self.order[(place + 1) % self.pairs]
            for lane in range(2):
                self.ahead.append((2 * pair + lane, 2 * following + lane))
                self.behind.append((2 * following + lane, 2 * pair + lane))
        self.across = [(device, device ^ 1) for device in range(size)]

    def slots(self):
        offsets = [(0, 0), (0, 1)]
        for step in range(1, self.reach):
            offsets += [(-step, 0), (step, 0), (-step, 1), (step, 1)]
        offsets += [(self.reach, 0), (self.reach, 1)]
        table = np.zeros((self.size, self.size), np.int32)
        for device in range(self.size):
            place = self.order.index(device // 2)
            for slot, (offset, flip) in enumerate(offsets):
                pair = self.order[(place + offset) % self.pairs]
                table[device, 2 * pair + (device % 2 ^ flip)] = slot
        return table

    def forward(self, array):
        return lax.ppermute(array, "wide", self.ahead)

    def backward(self, array):
        return lax.ppermute(array, "wide", self.behind)

    def twin(self, array):
        return lax.ppermute(array, "wide", self.across)

    def gather(self, rows, groups):
        groups.append([rows, self.twin(rows)])
        ahead = behind = rows
        middle = rows.shape[0] // 2
        for step in range(1, self.reach + 1):
            if step == self.reach:
                ahead, behind = ahead[:middle], behind[middle:]
            (ahead, behind), _ = yield ((self.forward, ahead), (self.backward, behind)), ()
            groups.append([ahead, behind, self.twin(ahead), self.twin(behind)])

    def scatter(self, make):
        def pair_sum(step, *held):
            mine, other = make(step, *held)
            return mine + self.twin(other.astype(jnp.bfloat16)).astype(jnp.float32)

        total = pair_sum(self.reach)
        middle = total.shape[0] // 2
        low, high = total[:middle], total[middle:]
        for step in range(self.reach - 1, -1, -1):
            held = (low.astype(jnp.bfloat16), high.astype(jnp.bfloat16))
            (down, up), (total,) = (
                yield (
                    ((self.backward, held[0]), (self.forward, held[1])),
                    (pair_sum(step, *held),),
                )
            )
            down, up = down.astype(jnp.float32), up.astype(jnp.float32)
            if step == 0:
                return total + down + up
            count = total.shape[0] // 2
            low, high = total[:count], total[count:]
            if step == self.reach - 1:
                low = jnp.concatenate([low[:middle] + down, low[middle:]], axis=0)
                high = jnp.concatenate([high[:middle], high[middle:] + up], axis=0)
            else:
                low, high = low + down, high + up

    def total(self, array):
        def flip(bit):
            pairs = [(i, i ^ bit) for i in range(self.size)]
            return functools.partial(lax.ppermute, axis_name="wide", perm=pairs)

        ways = [swapped]
        bit = 4
        while bit < self.size:
            ways.insert(0 if bit > 4 else 1, flip(bit))
            bit *= 2
        for way in ways:
            ((other,), _) = yield ((way, array),), ()
            array = array + other
        for bit in (2, 1):
            array = array + flip(bit)(array)
        return array


class Stream:
    def __init__(self, hops):
        self.hops = hops
        self.asked, self.beside = next(hops)
        self.result = None

    def post(self):
        return [send(array) for send, array in self.asked]

    def land(self, arrived, beside):
        try:
            self.asked, self.beside = self.hops.send((arrived, beside))
        except StopIteration as end:
            self.asked, self.beside = None, ()
            self.result = end.value


class Swaps:
    def __init__(self):
        self.waiting = []
        self.done = {}
        self.parts = {}

    def add(self, name, parts):
        self.parts[name] = list(parts)
        self.done[name] = []
        self.waiting += [(name, index) for index in range(len(parts))]

    def sums(self, name):
        return (self.parts[name], self.done[name])


def joined(*lists):
    held = list(lax.optimization_barrier(tuple(array for part in lists for array in part)))
    result = []
    for part in lists:
        result.append(held[: len(part)])
        held = held[len(part) :]
    return result


def hop(streams, swaps=None, count=1, beside=(), work=None, given=()):
    streams = [stream for stream in streams if stream.asked is not None]
    ready = []
    if swaps is not None:
        ready, swaps.waiting = swaps.waiting[:count], swaps.waiting[count:]
    asked = [array for stream in streams for _, array in stream.asked]
    if work is not None:
        flat, tree = jax.tree.flatten(given)
        beside = work(*jax.tree.unflatten(tree, joined(asked, flat)[1]))
    pieces = joined(asked, [swaps.parts[name][index] for name, index in ready])[1]
    lists = [stream.post() for stream in streams]
    lists += [stream.beside for stream in streams]
    lists.append([swapped(piece) for piece in pieces])
    lists.append(beside)
    *lists, moved, beside = joined(*lists)
    for (name, _), piece in zip(ready, moved):
        swaps.done[name].append(piece)
    for place, stream in enumerate(streams):
        stream.land(lists[place], lists[len(streams) + place])
    return beside


def travel(stream, swaps=None, count=1):
    while stream.asked is not None:
        hop([stream], swaps, count)
    return stream.result


def swapped(part):
    return lax.ppermute(part, "narrow", [(0, 1), (1, 0)])


def after(array, *others):
    return lax.optimization_barrier((array,) + others)[0]


def halves(array):
    middle = array.shape[0] // 2
    return array[:middle], array[middle:]


def shards(
    ring,
    layer_input,
    lengths,
    attn_gain,
    w_query,
    w_key,
    w_value,
    w_out,
    mlp_gain,
    w_gate,
    w_up,
    w_down,
    cotangent,
):
    size = ring.size
    local_rows = layer_input.shape[1]
    model_width = layer_input.shape[2]
    row_count = local_rows * size
    own_width = model_width // size
    width = max(own_width, 2 * HEAD_DIM)
    sharing = width // own_width
    device = lax.axis_index("wide")
    member = device % sharing
    slot_of = lax.dynamic_index_in_dim(jnp.asarray(ring.slots()), device, keepdims=False)

    def own_columns(array):
        if sharing == 1:
            return array
        runs = array.reshape(array.shape[0], -1, sharing, own_width)
        return lax.dynamic_index_in_dim(runs, member, axis=2, keepdims=False).reshape(
            array.shape[0], -1
        )

    positions = device * local_rows + jnp.arange(local_rows, dtype=jnp.int32)
    valid_rows = (positions < lengths[0]).astype(jnp.float32)[:, None]
    cosine, sine = rotary_tables(row_count, width)
    inputs = layer_input[0].astype(jnp.float32)
    gain_one = attn_gain.astype(jnp.float32)
    gain_two = mlp_gain.astype(jnp.float32)
    y_back = cotangent[0].astype(jnp.float32) * valid_rows
    mlp_back = y_back.astype(jnp.bfloat16)

    blocks = jnp.concatenate(
        [w.reshape(own_width, -1, width) for w in (w_query, w_key, w_value)], axis=-1
    ).transpose(1, 0, 2)
    blocks = jnp.repeat(blocks, sharing, axis=0)
    half_rows = own_width // 2
    upper = lax.axis_index("narrow") == 1
    w_out_heads = w_out
    if sharing > 1:
        near = [list(range(a, a + sharing)) for a in range(0, size, sharing)]
        w_out_heads = lax.all_gather(w_out, "wide", axis=0, tiled=True, axis_index_groups=near)
    units = w_gate.shape[0]
    w_both = jnp.concatenate([w_gate, w_up], axis=0)
    factor_one = rms_factor(inputs)
    normed_one = inputs * factor_one
    norm_one = (normed_one * gain_one).astype(jnp.bfloat16)
    sent = jnp.where(upper, blocks[:, half_rows:], blocks[:, :half_rows])
    near_half = lax.all_to_all(after(sent, norm_one), "wide", 0, 0, tiled=True)
    group_one = []
    one = Stream(ring.gather(norm_one, group_one))
    hop([one])
    cosine, sine = hop([one], beside=(cosine, sine))
    while one.asked is not None:
        hop([one])
    far_half = swapped(near_half)
    w_heads = jnp.stack(
        [jnp.where(upper, far_half, near_half), jnp.where(upper, near_half, far_half)], axis=1
    ).reshape(model_width, 3 * width)
    pieces_one = sum(group_one, [])
    lin = dot_nn(jnp.concatenate(pieces_one, axis=0), w_heads)
    starts = [0]
    for rows in group_one:
        starts.append(starts[-1] + sum(piece.shape[0] for piece in rows))

    def group_of(array, step):
        return array[starts[step] : starts[step + 1]]

    group_back = []
    back = Stream(ring.gather(after(mlp_back, lin), group_back))
    heads_attention, query, key, value, logs = hop(
        [back], beside=attention_forward(slot_of, lengths, lin, cosine, sine)
    )
    attention = own_columns(heads_attention)

    def residual_part(step, *held):
        mine, other = halves(group_of(attention, step))
        return dot_nn(mine, w_out), dot_nn(other, w_out)

    mixed = Stream(ring.scatter(residual_part))
    while mixed.asked is not None:
        hop([mixed, back])
    residual = inputs + mixed.result
    factor_two = rms_factor(residual)
    normed_two = residual * factor_two
    norm_two = (normed_two * gain_two).astype(jnp.bfloat16)
    group_two = []
    two = Stream(ring.gather(norm_two, group_two))
    hidden = []
    both_back = []

    def feed(step):
        both = dot_nt(jnp.concatenate(group_two[step], axis=0), w_both)
        gate_proj, up_proj = both[:, :units], both[:, units:]
        hidden_back = dot_nt(jnp.concatenate(group_back[step], axis=0), w_down)
        return (
            (jax.nn.silu(gate_proj) * up_proj).astype(jnp.bfloat16),
            jnp.concatenate(swiglu_back(hidden_back, gate_proj, up_proj), axis=1),
        )

    for step in range(ring.reach):
        fed = hop([two], beside=feed(step))
        hidden.append(fed[0])
        both_back.append(fed[1])
    fed = feed(ring.reach)
    hidden.append(fed[0])
    both_back.append(fed[1])

    def pull_part(step, *held):
        mine, other = halves(after(both_back[step], *held))
        return dot_nn(mine, w_both), dot_nn(other, w_both)

    def mlp_part(step, *held):
        mine, other = halves(after(hidden[step], *(held or (branch_back,))))
        return dot_nn(mine, w_down), dot_nn(other, w_down)

    swaps = Swaps()
    cuts = [[units // 16 * count for count in row] for row in ((4, 4, 8), (8, 8), (2, 8, 4, 2))]
    pull = Stream(ring.scatter(pull_part))
    hop([pull])
    swaps.add(
        "down",
        hop(
            [pull],
            work=functools.partial(weight_grads, cuts=cuts[0]),
            given=(hidden, sum(group_back, [])),
        ),
    )
    norm_two_back = travel(pull, swaps)
    residual_back = y_back + norm_back(norm_two_back, normed_two, gain_two, factor_two)
    gain_two_term = jnp.sum(norm_two_back * normed_two, axis=0)
    branch_back = residual_back.astype(jnp.bfloat16)
    mlp = Stream(ring.scatter(mlp_part))
    group_branch = []
    branch = Stream(ring.gather(branch_back, group_branch))
    pieces_two = sum(group_two, [])
    for place, name in enumerate(("gate", "up")):
        parts = hop(
            [branch, mlp],
            swaps,
            work=functools.partial(
                weight_grads, cuts=cuts[1 + place], place=place
            ),
            given=(both_back, pieces_two),
        )
        swaps.add(name, parts)
    (down_sum,) = hop([branch, mlp], swaps, work=sum_pieces, given=swaps.sums("down"))
    while branch.asked is not None:
        hop([branch], swaps)
    upstream = jnp.concatenate(
        [
            dot_nt(jnp.concatenate(rows, axis=0), w_out_heads).astype(jnp.bfloat16)
            for rows in group_branch
        ],
        axis=0,
    )
    group_rows = [stop - start for start, stop in zip(starts, starts[1:])]
    lin_back = hop(
        [mlp],
        swaps,
        beside=attention_backward(
            slot_of,
            lengths,
            query,
            key,
            value,
            heads_attention,
            upstream,
            logs,
            cosine,
            sine,
            group_rows,
        ),
    )
    lin_back = [own_columns(rows) for rows in lin_back]
    w_own = own_columns(w_heads)

    def input_part(step, *held):
        mine, other = halves(after(lin_back[step], *held))
        return dot_nt(mine, w_own), dot_nt(other, w_own)

    pulled = Stream(ring.scatter(input_part))
    side = lax.axis_index("narrow").reshape(1)
    keep, give, gain_one_sum = hop(
        [pulled],
        swaps,
        work=functools.partial(heads_grads, rows=own_width),
        given=(pieces_one, lin_back, w_own, side),
    )
    while mlp.asked is not None:
        hop([mlp])
    totals = Stream(ring.total(jnp.stack([gain_one_sum[0] / gain_one, gain_two_term])))

    def before(piece, left, rights, parts, others):
        return (
            swapped(piece),
            *weight_grads([left], rights, (own_width,)),
            *sum_pieces(parts, others),
        )

    given, out_part, gate_sum = hop(
        [pulled, totals],
        work=before,
        given=(give, attention, sum(group_branch, []), *swaps.sums("gate")),
    )
    heads_sum = lax.all_to_all(
        (keep.astype(jnp.float32) + given.astype(jnp.float32)).astype(jnp.bfloat16),
        "wide",
        0,
        0,
        tiled=True,
    )
    swaps.add("out", [out_part])
    hop([pulled, totals], swaps)
    (up_sum,) = hop([pulled, totals], swaps, work=sum_pieces, given=swaps.sums("up"))
    while pulled.asked is not None or totals.asked is not None:
        hop([pulled, totals])
    norm_one_back = pulled.result
    block_output = (residual + after(mlp.result, norm_one_back)).astype(jnp.bfloat16)
    gain_totals = totals.result
    far = swapped(heads_sum)
    (out_sum,) = sum_pieces(*swaps.sums("out"))
    attention_sums = assemble([heads_sum], [far], side)
    input_back = residual_back + norm_back(norm_one_back, normed_one, gain_one, factor_one)
    return (
        block_output[None],
        input_back[None],
        gain_totals[0],
        attention_sums[0],
        attention_sums[1],
        attention_sums[2],
        out_sum,
        gain_totals[1],
        gate_sum,
        up_sum,
        down_sum,
    )


def solution(mesh):
    placed = (
        P("narrow", "wide", None),
        P("narrow"),
        P(),
        P("wide", None),
        P("wide", None),
        P("wide", None),
        P("wide", None),
        P(),
        P("wide", None),
        P("wide", None),
        P("wide", None),
        P("narrow", "wide", None),
    )
    return jax.shard_map(
        functools.partial(shards, Ring(mesh.shape["wide"])),
        mesh=mesh,
        in_specs=placed,
        out_specs=(
            P("narrow", "wide", None),
            P("narrow", "wide", None),
            P(),
            P("wide", None),
            P("wide", None),
            P("wide", None),
            P("wide", None),
            P(),
            P("wide", None),
            P("wide", None),
            P("wide", None),
        ),
        check_vma=False,
    )
```

```python
import functools
import jax
import jax.numpy as jnp
from jax import lax
from jax.experimental import pallas as pl
from jax.experimental.pallas import tpu as pltpu
import math
import numpy as np
from jax.sharding import PartitionSpec as P

HEAD_DIM = 64
NEGATIVE = -1e30
VMEM_LIMIT = 56 * 1024 * 1024


def dot_nt(a, b):
    return lax.dot_general(a, b, (((1,), (1,)), ((), ())), preferred_element_type=jnp.float32)


def dot_nn(a, b):
    return lax.dot_general(a, b, (((1,), (0,)), ((), ())), preferred_element_type=jnp.float32)


def half_turn(tensor):
    width = tensor.shape[-1]
    half_dim = HEAD_DIM // 2
    lane = lax.broadcasted_iota(jnp.int32, tensor.shape, 1)
    return jnp.where(
        lane % HEAD_DIM < half_dim,
        -pltpu.roll(tensor, width - half_dim, 1),
        pltpu.roll(tensor, half_dim, 1),
    )


def head_lanes(block, head):
    lane = lax.broadcasted_iota(jnp.int32, block.shape, 1)
    return jnp.where(lane // HEAD_DIM == head, block, jnp.zeros_like(block))


def forward_kernel(
    slot_ref, length_ref, lin_ref, cos_ref, sin_ref,
    att_ref, query_ref, key_ref, value_ref, log_ref,
    turned, attn_nat,
):
    rows = query_ref.shape[0]
    width = query_ref.shape[1]
    heads = width // HEAD_DIM
    slots = slot_ref.shape[0]
    shard = rows // slots
    length = length_ref[0]
    scale = HEAD_DIM ** (-0.5)

    @pl.loop(0, slots, unroll=4)
    def _(place):
        source = pl.ds(pl.multiple_of(slot_ref[place] * shard, shard), shard)
        target = pl.ds(pl.multiple_of(place * shard, shard), shard)
        cosine = cos_ref[target, :]
        sine = sin_ref[target, :]
        query_lin = lin_ref[source, 0:width]
        key_lin = lin_ref[source, width : 2 * width]
        value_lin = lin_ref[source, 2 * width : 3 * width]
        query = (query_lin * cosine + half_turn(query_lin) * sine).astype(jnp.bfloat16)
        query_ref[target, :] = (query.astype(jnp.float32) * scale).astype(jnp.bfloat16)
        key_ref[target, :] = (key_lin * cosine + half_turn(key_lin) * sine).astype(jnp.bfloat16)
        value_ref[target, :] = value_lin.astype(jnp.bfloat16)
        turned[:, target] = value_lin.T.astype(jnp.bfloat16)

    block_q = min(1024, rows)
    block_k = min(512, rows)

    @pl.loop(0, rows // block_q)
    def _(i):
        q_first = pl.multiple_of(i * block_q, block_q)
        query = query_ref[pl.ds(q_first, block_q), :]
        parts = [head_lanes(query, h) for h in range(heads)]
        q_pos = q_first + lax.broadcasted_iota(jnp.int32, (1, block_q), 1)
        limit = jnp.minimum(q_pos, length - 1)
        full = jnp.minimum(q_first, length) // block_k
        stop = (jnp.minimum(q_first + block_q, length) + block_k - 1) // block_k

        def step(j, state, masked):
            k_first = pl.multiple_of(j * block_k, block_k)
            key = key_ref[pl.ds(k_first, block_k), :]
            out = []
            if masked:
                k_pos = k_first + lax.broadcasted_iota(jnp.int32, (block_k, block_q), 0)
                allowed = k_pos <= limit
            for h in range(heads):
                best, total, acc = state[3 * h : 3 * h + 3]
                scores = dot_nt(key, parts[h])
                if masked:
                    scores = jnp.where(allowed, scores, NEGATIVE)
                new_best = jnp.maximum(best, jnp.max(scores, axis=0, keepdims=True))
                weight = jnp.exp(scores - new_best)
                shrink = jnp.exp(best - new_best)
                total = total * shrink + jnp.sum(weight, axis=0, keepdims=True)
                value_t = turned[h * HEAD_DIM : (h + 1) * HEAD_DIM, pl.ds(k_first, block_k)]
                acc = acc * shrink + dot_nn(value_t, weight.astype(jnp.bfloat16))
                out += [new_best, total, acc]
            return tuple(out)

        state = ()
        for h in range(heads):
            state += (
                jnp.full((1, block_q), NEGATIVE, jnp.float32),
                jnp.zeros((1, block_q), jnp.float32),
                jnp.zeros((HEAD_DIM, block_q), jnp.float32),
            )
        state = lax.fori_loop(0, full, functools.partial(step, masked=False), state)
        state = lax.fori_loop(full, stop, functools.partial(step, masked=True), state)
        for h in range(heads):
            best, total, acc = state[3 * h : 3 * h + 3]
            log_ref[h : h + 1, pl.ds(q_first, block_q)] = best + jnp.log(total)
        joined = jnp.concatenate([state[3 * h + 2] / state[3 * h + 1] for h in range(heads)], axis=0)
        attn_nat[pl.ds(q_first, block_q), :] = joined.T.astype(jnp.bfloat16)

    @pl.loop(0, slots, unroll=4)
    def _(place):
        source = pl.ds(pl.multiple_of(slot_ref[place] * shard, shard), shard)
        target = pl.ds(pl.multiple_of(place * shard, shard), shard)
        att_ref[source, :] = attn_nat[target, :]


def attention_forward(slot_of, length, lin, cosine, sine):
    rows, width = cosine.shape
    vmem = pl.BlockSpec(memory_space=pltpu.VMEM)
    smem = pl.BlockSpec(memory_space=pltpu.SMEM)
    half = jax.ShapeDtypeStruct((rows, width), jnp.bfloat16)
    return pl.pallas_call(
        forward_kernel,
        out_shape=(half, half, half, half, jax.ShapeDtypeStruct((8, rows), jnp.float32)),
        in_specs=[smem, smem, vmem, vmem, vmem],
        out_specs=(vmem,) * 5,
        scratch_shapes=[
            pltpu.VMEM((width, rows), jnp.bfloat16),
            pltpu.VMEM((rows, width), jnp.bfloat16),
        ],
        compiler_params=pltpu.CompilerParams(vmem_limit_bytes=VMEM_LIMIT),
        cost_estimate=pl.CostEstimate(
            flops=4 * rows * rows * width, bytes_accessed=24 * rows * width, transcendentals=rows * rows
        ),
        name="attention_forward",
    )(slot_of, length, lin, cosine, sine)


def backward_kernel(
    slot_ref, length_ref, query_ref, key_ref, value_ref, att_ref, up_ref, log_ref, cos_ref, sin_ref,
    *refs,
):
    *out_refs, out_ref, key_t, up_nat, delta, key_acc, value_acc, query_acc = refs
    rows = query_ref.shape[0]
    width = query_ref.shape[1]
    heads = width // HEAD_DIM
    slots = slot_ref.shape[0]
    shard = rows // slots
    length = length_ref[0]
    scale = HEAD_DIM ** (-0.5)
    key_acc[...] = jnp.zeros_like(key_acc)
    value_acc[...] = jnp.zeros_like(value_acc)

    @pl.loop(0, slots, unroll=4)
    def _(place):
        source = pl.ds(pl.multiple_of(slot_ref[place] * shard, shard), shard)
        target = pl.ds(pl.multiple_of(place * shard, shard), shard)
        upstream = up_ref[source, :]
        up_nat[target, :] = upstream
        product = (upstream.astype(jnp.float32) * att_ref[source, :].astype(jnp.float32)).T
        for h in range(heads):
            delta[h : h + 1, target] = jnp.sum(
                product[h * HEAD_DIM : (h + 1) * HEAD_DIM, :], axis=0, keepdims=True
            )
        key_t[:, target] = key_ref[target, :].astype(jnp.float32).T.astype(jnp.bfloat16)

    block_q = min(512, rows)
    block_k = min(512, rows)

    @pl.loop(0, rows // block_q)
    def _(i):
        q_first = pl.multiple_of(i * block_q, block_q)
        here = pl.ds(q_first, block_q)
        query = query_ref[here, :]
        upstream = up_nat[here, :]
        q_parts = [head_lanes(query, h) for h in range(heads)]
        u_parts = [head_lanes(upstream, h) for h in range(heads)]
        logs = [log_ref[h : h + 1, here] for h in range(heads)]
        deltas = [delta[h : h + 1, here] for h in range(heads)]
        q_pos = q_first + lax.broadcasted_iota(jnp.int32, (1, block_q), 1)
        limit = jnp.minimum(q_pos, length - 1)
        full = jnp.minimum(q_first, length) // block_k
        stop = (jnp.minimum(q_first + block_q, length) + block_k - 1) // block_k

        def step(j, state, masked):
            k_first = pl.multiple_of(j * block_k, block_k)
            there = pl.ds(k_first, block_k)
            key = key_ref[there, :]
            value = value_ref[there, :]
            if masked:
                k_pos = k_first + lax.broadcasted_iota(jnp.int32, (block_k, block_q), 0)
                allowed = k_pos <= limit
            out = []
            key_add = None
            for h in range(heads):
                prob = jnp.exp(dot_nt(key, q_parts[h]) - logs[h])
                if masked:
                    prob = jnp.where(allowed, prob, 0.0)
                pulled = dot_nt(value, u_parts[h])
                score_back = (prob * (pulled - deltas[h])).astype(jnp.bfloat16)
                one = dot_nn(prob.astype(jnp.bfloat16), u_parts[h])
                two = dot_nn(score_back, q_parts[h])
                value_add = one if key_add is None else value_add + one
                key_add = two if key_add is None else key_add + two
                out.append(
                    state[h] + dot_nn(key_t[h * HEAD_DIM : (h + 1) * HEAD_DIM, there], score_back)
                )
            value_acc[there, :] += value_add
            key_acc[there, :] += key_add
            return tuple(out)

        state = tuple(jnp.zeros((HEAD_DIM, block_q), jnp.float32) for h in range(heads))
        state = lax.fori_loop(0, full, functools.partial(step, masked=False), state)
        state = lax.fori_loop(full, stop, functools.partial(step, masked=True), state)
        query_acc[here, :] = (jnp.concatenate(state, axis=0) * scale).T

    @pl.loop(0, slots, unroll=4)
    def _(place):
        source = pl.ds(pl.multiple_of(slot_ref[place] * shard, shard), shard)
        target = pl.ds(pl.multiple_of(place * shard, shard), shard)
        cosine = cos_ref[target, :]
        sine = sin_ref[target, :]
        for piece, held in enumerate((query_acc, key_acc)):
            grad = held[target, :]
            out_ref[source, piece * width : (piece + 1) * width] = (
                grad * cosine - half_turn(grad * sine)
            ).astype(jnp.bfloat16)
        out_ref[source, 2 * width : 3 * width] = value_acc[target, :].astype(jnp.bfloat16)

    start = 0
    for group_ref in out_refs:
        count = group_ref.shape[0]
        group_ref[...] = out_ref[start : start + count, :]
        start += count


def attention_backward(
    slot_of, length, query, key, value, att, upstream, logs, cosine, sine, group_rows
):
    rows, width = query.shape
    vmem = pl.BlockSpec(memory_space=pltpu.VMEM)
    smem = pl.BlockSpec(memory_space=pltpu.SMEM)
    return pl.pallas_call(
        backward_kernel,
        out_shape=[
            jax.ShapeDtypeStruct((count, 3 * width), jnp.bfloat16) for count in group_rows
        ],
        in_specs=[smem, smem] + [vmem] * 8,
        out_specs=[vmem] * len(group_rows),
        scratch_shapes=[
            pltpu.VMEM((rows, 3 * width), jnp.bfloat16),
            pltpu.VMEM((width, rows), jnp.bfloat16),
            pltpu.VMEM((rows, width), jnp.bfloat16),
            pltpu.VMEM((8, rows), jnp.float32),
            pltpu.VMEM((rows, width), jnp.float32),
            pltpu.VMEM((rows, width), jnp.float32),
            pltpu.VMEM((rows, width), jnp.float32),
        ],
        compiler_params=pltpu.CompilerParams(vmem_limit_bytes=VMEM_LIMIT),
        cost_estimate=pl.CostEstimate(
            flops=10 * rows * rows * width, bytes_accessed=36 * rows * width, transcendentals=rows * rows
        ),
        name="attention_backward",
    )(slot_of, length, query, key, value, att, upstream, logs, cosine, sine)


EPSILON = 1e-05
THETA = 130000.0


def contract_rows(left_side, right_side):
    return lax.dot_general(
        left_side, right_side, (((0,), (0,)), ((), ())), preferred_element_type=jnp.float32
    )


def rotary_tables(row_count, width):
    half_dim = HEAD_DIM // 2
    feature = (jnp.arange(width, dtype=jnp.int32) % half_dim).astype(jnp.float32)
    frequency = THETA ** (-feature * 2.0 / HEAD_DIM)
    angles = jnp.arange(row_count, dtype=jnp.float32)[:, None] * frequency[None, :]
    return (jnp.cos(angles), jnp.sin(angles))


def rms_factor(matrix):
    return lax.rsqrt(jnp.mean(matrix * matrix, axis=-1, keepdims=True) + EPSILON)


def norm_back(upstream, normed, gain_vec, factor):
    scaled = upstream * gain_vec
    return factor * (scaled - normed * jnp.mean(scaled * normed, axis=-1, keepdims=True))


def swiglu_back(hidden_back, gate_proj, up_proj):
    sigmoid_gate = jax.nn.sigmoid(gate_proj)
    gate_back = hidden_back * up_proj * sigmoid_gate * (1.0 + gate_proj * (1.0 - sigmoid_gate))
    up_back = hidden_back * jax.nn.silu(gate_proj)
    return (gate_back.astype(jnp.bfloat16), up_back.astype(jnp.bfloat16))


SMALL = pl.CostEstimate(flops=1024, bytes_accessed=1024, transcendentals=0)


def dot_tn(a, b):
    return lax.dot_general(a, b, (((0,), (0,)), ((), ())), preferred_element_type=jnp.float32)


def fitting(tile, extent):
    return math.gcd(tile, extent)


def first(i):
    return (0, 0)


def along(i):
    return (0, i)


def down_rows(i):
    return (i, 0)


def fill(target_ref, piece_refs):
    start = 0
    for piece_ref in piece_refs:
        count = piece_ref.shape[0]
        target_ref[start : start + count, :] = piece_ref[...]
        start += count


def grads_kernel(lefts, rights, *refs):
    out_refs, (left_ref, right_ref) = refs[lefts + rights : -2], refs[-2:]

    @pl.when(pl.program_id(0) == 0)
    def _():
        fill(left_ref, refs[:lefts])

    fill(right_ref, refs[lefts : lefts + rights])
    total = dot_tn(left_ref[...], right_ref[...])
    start = 0
    for out_ref in out_refs:
        rows = out_ref.shape[0]
        out_ref[...] = total[start : start + rows].astype(jnp.bfloat16)
        start += rows


def weight_grads(lefts, rights, cuts, place=0):
    count = sum(piece.shape[0] for piece in lefts)
    wide = sum(cuts)
    width = rights[0].shape[1]
    tile = fitting(512, width)
    return pl.pallas_call(
        functools.partial(grads_kernel, len(lefts), len(rights)),
        grid=(width // tile,),
        in_specs=[pl.BlockSpec((piece.shape[0], wide), lambda i: (0, place)) for piece in lefts]
        + [pl.BlockSpec((piece.shape[0], tile), along) for piece in rights],
        out_specs=[pl.BlockSpec((rows, tile), along) for rows in cuts],
        out_shape=[jax.ShapeDtypeStruct((rows, width), jnp.bfloat16) for rows in cuts],
        scratch_shapes=[
            pltpu.VMEM((count, wide), jnp.bfloat16),
            pltpu.VMEM((count, tile), jnp.bfloat16),
        ],
        compiler_params=pltpu.CompilerParams(vmem_limit_bytes=VMEM_LIMIT),
        cost_estimate=SMALL,
        name="weight_grads",
    )(*lefts, *rights)


def heads_kernel(rights, upper_ref, weight_ref, *refs):
    *piece_refs, keep_ref, give_ref, gain_ref, left_ref, right_ref = refs

    @pl.when(pl.program_id(0) == 0)
    def _():
        fill(right_ref, piece_refs[:rights])

    fill(left_ref, piece_refs[rights:])
    total = dot_tn(left_ref[...], right_ref[...])
    count, half, width = keep_ref.shape
    sums = jnp.sum(total * weight_ref[...].astype(jnp.float32), axis=1, keepdims=True)
    gain_ref[...] = jnp.broadcast_to(sums, (total.shape[0], 128)).T[:1]
    blocks = total.astype(jnp.bfloat16).reshape(count, 2, half, width)
    upper = upper_ref[0] == 1
    keep_ref[...] = jnp.where(upper, blocks[:, 1], blocks[:, 0])
    give_ref[...] = jnp.where(upper, blocks[:, 0], blocks[:, 1])


def heads_grads(lefts, rights, weight, upper, rows):
    count = sum(piece.shape[0] for piece in rights)
    wide, width = weight.shape
    tile = fitting(512, wide)
    half = ((tile // rows, rows // 2, width), lambda i: (i, 0, 0))
    whole = ((wide // rows, rows // 2, width), jnp.bfloat16)
    return pl.pallas_call(
        functools.partial(heads_kernel, len(rights)),
        grid=(wide // tile,),
        in_specs=[
            pl.BlockSpec(memory_space=pltpu.SMEM),
            pl.BlockSpec((tile, width), down_rows),
        ]
        + [pl.BlockSpec(piece.shape, first) for piece in rights]
        + [pl.BlockSpec((piece.shape[0], tile), along) for piece in lefts],
        out_specs=[pl.BlockSpec(*half), pl.BlockSpec(*half), pl.BlockSpec((1, tile), along)],
        out_shape=[
            jax.ShapeDtypeStruct(*whole),
            jax.ShapeDtypeStruct(*whole),
            jax.ShapeDtypeStruct((1, wide), jnp.float32),
        ],
        scratch_shapes=[
            pltpu.VMEM((count, tile), jnp.bfloat16),
            pltpu.VMEM((count, width), jnp.bfloat16),
        ],
        compiler_params=pltpu.CompilerParams(vmem_limit_bytes=VMEM_LIMIT),
        cost_estimate=SMALL,
        name="heads_grads",
    )(upper, weight, *rights, *lefts)


def assemble_kernel(side_ref, *refs):
    out_refs = refs[-3:]
    given = (len(refs) - 3) // 2
    size, part, width = refs[0].shape
    columns = width // 3
    upper = side_ref[0] == 1
    for index, (near_ref, far_ref) in enumerate(zip(refs[:given], refs[given:-3])):
        low = jnp.where(upper, far_ref[...], near_ref[...]).astype(jnp.float32)
        high = jnp.where(upper, near_ref[...], far_ref[...]).astype(jnp.float32)
        for piece, out_ref in enumerate(out_refs):
            for source in range(size):
                place = slice(source * columns, (source + 1) * columns)
                taken = slice(piece * columns, (piece + 1) * columns)
                for start, block in ((index, low), (given + index, high)):
                    out_ref[start * part : (start + 1) * part, place] = block[source, :, taken]


def assemble(near, far, side):
    size, part, width = near[0].shape
    shape = (2 * len(near) * part, size * width // 3)
    vmem = pl.BlockSpec(memory_space=pltpu.VMEM)
    return pl.pallas_call(
        assemble_kernel,
        in_specs=[pl.BlockSpec(memory_space=pltpu.SMEM)] + [vmem] * (2 * len(near)),
        out_specs=[vmem] * 3,
        out_shape=[jax.ShapeDtypeStruct(shape, jnp.float32)] * 3,
        compiler_params=pltpu.CompilerParams(vmem_limit_bytes=VMEM_LIMIT),
        cost_estimate=SMALL,
        name="assemble",
    )(side, *near, *far)


def sums_kernel(*refs):
    out_ref = refs[-1]
    count = (len(refs) - 1) // 2
    start = 0
    for part_ref, other_ref in zip(refs[:count], refs[count:-1]):
        rows = part_ref.shape[0]
        out_ref[start : start + rows, :] = part_ref[...].astype(jnp.float32) + other_ref[
            ...
        ].astype(jnp.float32)
        start += rows


def sum_pieces(parts, others):
    width = parts[0].shape[1]
    tile = fitting(512, width)
    total = sum(piece.shape[0] for piece in parts)
    return pl.pallas_call(
        sums_kernel,
        grid=(width // tile,),
        in_specs=[pl.BlockSpec((piece.shape[0], tile), along) for piece in (*parts, *others)],
        out_specs=[pl.BlockSpec((total, tile), along)],
        out_shape=[jax.ShapeDtypeStruct((total, width), jnp.float32)],
        compiler_params=pltpu.CompilerParams(vmem_limit_bytes=VMEM_LIMIT),
        cost_estimate=SMALL,
        name="sum_pieces",
    )(*parts, *others)


class Ring:
    def __init__(self, size):
        self.size = size
        self.pairs = size // 2
        self.reach = self.pairs // 2
        columns = self.pairs // 2
        self.order = [2 * a for a in range(columns)] + [2 * a + 1 for a in reversed(range(columns))]
        self.ahead = []
        self.behind = []
        for place, pair in enumerate(self.order):
            following = self.order[(place + 1) % self.pairs]
            for lane in range(2):
                self.ahead.append((2 * pair + lane, 2 * following + lane))
                self.behind.append((2 * following + lane, 2 * pair + lane))
        self.across = [(device, device ^ 1) for device in range(size)]

    def slots(self):
        offsets = [(0, 0), (0, 1)]
        for step in range(1, self.reach):
            offsets += [(-step, 0), (step, 0), (-step, 1), (step, 1)]
        offsets += [(self.reach, 0), (self.reach, 1)]
        table = np.zeros((self.size, self.size), np.int32)
        for device in range(self.size):
            place = self.order.index(device // 2)
            for slot, (offset, flip) in enumerate(offsets):
                pair = self.order[(place + offset) % self.pairs]
                table[device, 2 * pair + (device % 2 ^ flip)] = slot
        return table

    def forward(self, array):
        return lax.ppermute(array, "wide", self.ahead)

    def backward(self, array):
        return lax.ppermute(array, "wide", self.behind)

    def twin(self, array):
        return lax.ppermute(array, "wide", self.across)

    def gather(self, rows, groups):
        groups.append([rows, self.twin(rows)])
        ahead = behind = rows
        middle = rows.shape[0] // 2
        for step in range(1, self.reach + 1):
            if step == self.reach:
                ahead, behind = ahead[:middle], behind[middle:]
            (ahead, behind), _ = yield ((self.forward, ahead), (self.backward, behind)), ()
            groups.append([ahead, behind, self.twin(ahead), self.twin(behind)])

    def scatter(self, make):
        def pair_sum(step, *held):
            mine, other = make(step, *held)
            return mine + self.twin(other.astype(jnp.bfloat16)).astype(jnp.float32)

        total = pair_sum(self.reach)
        middle = total.shape[0] // 2
        low, high = total[:middle], total[middle:]
        for step in range(self.reach - 1, -1, -1):
            held = (low.astype(jnp.bfloat16), high.astype(jnp.bfloat16))
            (down, up), (total,) = (
                yield (
                    ((self.backward, held[0]), (self.forward, held[1])),
                    (pair_sum(step, *held),),
                )
            )
            down, up = down.astype(jnp.float32), up.astype(jnp.float32)
            if step == 0:
                return total + down + up
            count = total.shape[0] // 2
            low, high = total[:count], total[count:]
            if step == self.reach - 1:
                low = jnp.concatenate([low[:middle] + down, low[middle:]], axis=0)
                high = jnp.concatenate([high[:middle], high[middle:] + up], axis=0)
            else:
                low, high = low + down, high + up

    def total(self, array):
        def flip(bit):
            pairs = [(i, i ^ bit) for i in range(self.size)]
            return functools.partial(lax.ppermute, axis_name="wide", perm=pairs)

        ways = [swapped]
        bit = 4
        while bit < self.size:
            ways.insert(0 if bit > 4 else 1, flip(bit))
            bit *= 2
        for way in ways:
            ((other,), _) = yield ((way, array),), ()
            array = array + other
        for bit in (2, 1):
            array = array + flip(bit)(array)
        return array


class Stream:
    def __init__(self, hops):
        self.hops = hops
        self.asked, self.beside = next(hops)
        self.result = None

    def post(self):
        return [send(array) for send, array in self.asked]

    def land(self, arrived, beside):
        try:
            self.asked, self.beside = self.hops.send((arrived, beside))
        except StopIteration as end:
            self.asked, self.beside = None, ()
            self.result = end.value


class Swaps:
    def __init__(self):
        self.waiting = []
        self.done = {}
        self.parts = {}

    def add(self, name, parts):
        self.parts[name] = list(parts)
        self.done[name] = []
        self.waiting += [(name, index) for index in range(len(parts))]

    def sums(self, name):
        return (self.parts[name], self.done[name])


def joined(*lists):
    held = list(lax.optimization_barrier(tuple(array for part in lists for array in part)))
    result = []
    for part in lists:
        result.append(held[: len(part)])
        held = held[len(part) :]
    return result


def hop(streams, swaps=None, count=1, beside=(), work=None, given=()):
    streams = [stream for stream in streams if stream.asked is not None]
    ready = []
    if swaps is not None:
        ready, swaps.waiting = swaps.waiting[:count], swaps.waiting[count:]
    asked = [array for stream in streams for _, array in stream.asked]
    if work is not None:
        flat, tree = jax.tree.flatten(given)
        beside = work(*jax.tree.unflatten(tree, joined(asked, flat)[1]))
    pieces = joined(asked, [swaps.parts[name][index] for name, index in ready])[1]
    lists = [stream.post() for stream in streams]
    lists += [stream.beside for stream in streams]
    lists.append([swapped(piece) for piece in pieces])
    lists.append(beside)
    *lists, moved, beside = joined(*lists)
    for (name, _), piece in zip(ready, moved):
        swaps.done[name].append(piece)
    for place, stream in enumerate(streams):
        stream.land(lists[place], lists[len(streams) + place])
    return beside


def travel(stream, swaps=None, count=1):
    while stream.asked is not None:
        hop([stream], swaps, count)
    return stream.result


def swapped(part):
    return lax.ppermute(part, "narrow", [(0, 1), (1, 0)])


def after(array, *others):
    return lax.optimization_barrier((array,) + others)[0]


def halves(array):
    middle = array.shape[0] // 2
    return array[:middle], array[middle:]


def shards(
    ring,
    layer_input,
    lengths,
    attn_gain,
    w_query,
    w_key,
    w_value,
    w_out,
    mlp_gain,
    w_gate,
    w_up,
    w_down,
    cotangent,
):
    size = ring.size
    local_rows = layer_input.shape[1]
    model_width = layer_input.shape[2]
    row_count = local_rows * size
    own_width = model_width // size
    width = max(own_width, 2 * HEAD_DIM)
    sharing = width // own_width
    device = lax.axis_index("wide")
    member = device % sharing
    slot_of = lax.dynamic_index_in_dim(jnp.asarray(ring.slots()), device, keepdims=False)

    def own_columns(array):
        if sharing == 1:
            return array
        runs = array.reshape(array.shape[0], -1, sharing, own_width)
        return lax.dynamic_index_in_dim(runs, member, axis=2, keepdims=False).reshape(
            array.shape[0], -1
        )

    positions = device * local_rows + jnp.arange(local_rows, dtype=jnp.int32)
    valid_rows = (positions < lengths[0]).astype(jnp.float32)[:, None]
    cosine, sine = rotary_tables(row_count, width)
    inputs = layer_input[0].astype(jnp.float32)
    gain_one = attn_gain.astype(jnp.float32)
    gain_two = mlp_gain.astype(jnp.float32)
    y_back = cotangent[0].astype(jnp.float32) * valid_rows
    mlp_back = y_back.astype(jnp.bfloat16)

    blocks = jnp.concatenate(
        [w.reshape(own_width, -1, width) for w in (w_query, w_key, w_value)], axis=-1
    ).transpose(1, 0, 2)
    blocks = jnp.repeat(blocks, sharing, axis=0)
    half_rows = own_width // 2
    upper = lax.axis_index("narrow") == 1
    w_out_heads = w_out
    if sharing > 1:
        near = [list(range(a, a + sharing)) for a in range(0, size, sharing)]
        w_out_heads = lax.all_gather(w_out, "wide", axis=0, tiled=True, axis_index_groups=near)
    units = w_gate.shape[0]
    w_both = jnp.concatenate([w_gate, w_up], axis=0)
    factor_one = rms_factor(inputs)
    normed_one = inputs * factor_one
    norm_one = (normed_one * gain_one).astype(jnp.bfloat16)
    sent = jnp.where(upper, blocks[:, half_rows:], blocks[:, :half_rows])
    near_half = lax.all_to_all(after(sent, norm_one), "wide", 0, 0, tiled=True)
    group_one = []
    one = Stream(ring.gather(norm_one, group_one))
    hop([one])
    cosine, sine = hop([one], beside=(cosine, sine))
    while one.asked is not None:
        hop([one])
    far_half = swapped(near_half)
    w_heads = jnp.stack(
        [jnp.where(upper, far_half, near_half), jnp.where(upper, near_half, far_half)], axis=1
    ).reshape(model_width, 3 * width)
    pieces_one = sum(group_one, [])
    lin = dot_nn(jnp.concatenate(pieces_one, axis=0), w_heads)
    starts = [0]
    for rows in group_one:
        starts.append(starts[-1] + sum(piece.shape[0] for piece in rows))

    def group_of(array, step):
        return array[starts[step] : starts[step + 1]]

    group_back = []
    back = Stream(ring.gather(after(mlp_back, lin), group_back))
    heads_attention, query, key, value, logs = hop(
        [back], beside=attention_forward(slot_of, lengths, lin, cosine, sine)
    )
    attention = own_columns(heads_attention)

    def residual_part(step, *held):
        mine, other = halves(group_of(attention, step))
        return dot_nn(mine, w_out), dot_nn(other, w_out)

    mixed = Stream(ring.scatter(residual_part))
    while mixed.asked is not None:
        hop([mixed, back])
    residual = inputs + mixed.result
    factor_two = rms_factor(residual)
    normed_two = residual * factor_two
    norm_two = (normed_two * gain_two).astype(jnp.bfloat16)
    group_two = []
    two = Stream(ring.gather(norm_two, group_two))
    hidden = []
    both_back = []

    def feed(step):
        both = dot_nt(jnp.concatenate(group_two[step], axis=0), w_both)
        gate_proj, up_proj = both[:, :units], both[:, units:]
        hidden_back = dot_nt(jnp.concatenate(group_back[step], axis=0), w_down)
        return (
            (jax.nn.silu(gate_proj) * up_proj).astype(jnp.bfloat16),
            jnp.concatenate(swiglu_back(hidden_back, gate_proj, up_proj), axis=1),
        )

    for step in range(ring.reach):
        fed = hop([two], beside=feed(step))
        hidden.append(fed[0])
        both_back.append(fed[1])
    fed = feed(ring.reach)
    hidden.append(fed[0])
    both_back.append(fed[1])

    def pull_part(step, *held):
        mine, other = halves(after(both_back[step], *held))
        return dot_nn(mine, w_both), dot_nn(other, w_both)

    def mlp_part(step, *held):
        mine, other = halves(after(hidden[step], *(held or (branch_back,))))
        return dot_nn(mine, w_down), dot_nn(other, w_down)

    swaps = Swaps()
    cuts = [[units // 16 * count for count in row] for row in ((4, 4, 8), (8, 8), (3, 9, 4))]
    pull = Stream(ring.scatter(pull_part))
    hop([pull])
    swaps.add(
        "down",
        hop(
            [pull],
            work=functools.partial(weight_grads, cuts=cuts[0]),
            given=(hidden, sum(group_back, [])),
        ),
    )
    norm_two_back = travel(pull, swaps)
    residual_back = y_back + norm_back(norm_two_back, normed_two, gain_two, factor_two)
    gain_two_term = jnp.sum(norm_two_back * normed_two, axis=0)
    branch_back = residual_back.astype(jnp.bfloat16)
    mlp = Stream(ring.scatter(mlp_part))
    group_branch = []
    branch = Stream(ring.gather(branch_back, group_branch))
    pieces_two = sum(group_two, [])
    for place, name in enumerate(("gate", "up")):
        parts = hop(
            [branch, mlp],
            swaps,
            work=functools.partial(
                weight_grads, cuts=cuts[1 + place], place=place
            ),
            given=(both_back, pieces_two),
        )
        swaps.add(name, parts)
    (down_sum,) = hop([branch, mlp], swaps, work=sum_pieces, given=swaps.sums("down"))
    while branch.asked is not None:
        hop([branch], swaps)
    upstream = jnp.concatenate(
        [
            dot_nt(jnp.concatenate(rows, axis=0), w_out_heads).astype(jnp.bfloat16)
            for rows in group_branch
        ],
        axis=0,
    )
    group_rows = [stop - start for start, stop in zip(starts, starts[1:])]
    lin_back = hop(
        [mlp],
        swaps,
        beside=attention_backward(
            slot_of,
            lengths,
            query,
            key,
            value,
            heads_attention,
            upstream,
            logs,
            cosine,
            sine,
            group_rows,
        ),
    )
    lin_back = [own_columns(rows) for rows in lin_back]
    w_own = own_columns(w_heads)

    def input_part(step, *held):
        mine, other = halves(after(lin_back[step], *held))
        return dot_nt(mine, w_own), dot_nt(other, w_own)

    pulled = Stream(ring.scatter(input_part))
    side = lax.axis_index("narrow").reshape(1)
    keep, give, gain_one_sum = hop(
        [pulled],
        swaps,
        work=functools.partial(heads_grads, rows=own_width),
        given=(pieces_one, lin_back, w_own, side),
    )
    while mlp.asked is not None:
        hop([mlp])
    totals = Stream(ring.total(jnp.stack([gain_one_sum[0] / gain_one, gain_two_term])))

    def before(piece, left, rights, parts, others):
        return (
            swapped(piece),
            *weight_grads([left], rights, (own_width,)),
            *sum_pieces(parts, others),
        )

    given, out_part, gate_sum = hop(
        [pulled, totals],
        work=before,
        given=(give, attention, sum(group_branch, []), *swaps.sums("gate")),
    )
    heads_sum = lax.all_to_all(
        (keep.astype(jnp.float32) + given.astype(jnp.float32)).astype(jnp.bfloat16),
        "wide",
        0,
        0,
        tiled=True,
    )
    swaps.add("out", [out_part])
    hop([pulled, totals], swaps)
    (up_sum,) = hop([pulled, totals], swaps, work=sum_pieces, given=swaps.sums("up"))
    while pulled.asked is not None or totals.asked is not None:
        hop([pulled, totals])
    norm_one_back = pulled.result
    block_output = (residual + after(mlp.result, norm_one_back)).astype(jnp.bfloat16)
    gain_totals = totals.result
    far = swapped(heads_sum)
    (out_sum,) = sum_pieces(*swaps.sums("out"))
    attention_sums = assemble([heads_sum], [far], side)
    input_back = residual_back + norm_back(norm_one_back, normed_one, gain_one, factor_one)
    return (
        block_output[None],
        input_back[None],
        gain_totals[0],
        attention_sums[0],
        attention_sums[1],
        attention_sums[2],
        out_sum,
        gain_totals[1],
        gate_sum,
        up_sum,
        down_sum,
    )


def solution(mesh):
    placed = (
        P("narrow", "wide", None),
        P("narrow"),
        P(),
        P("wide", None),
        P("wide", None),
        P("wide", None),
        P("wide", None),
        P(),
        P("wide", None),
        P("wide", None),
        P("wide", None),
        P("narrow", "wide", None),
    )
    return jax.shard_map(
        functools.partial(shards, Ring(mesh.shape["wide"])),
        mesh=mesh,
        in_specs=placed,
        out_specs=(
            P("narrow", "wide", None),
            P("narrow", "wide", None),
            P(),
            P("wide", None),
            P("wide", None),
            P("wide", None),
            P("wide", None),
            P(),
            P("wide", None),
            P("wide", None),
            P("wide", None),
        ),
        check_vma=False,
    )
```
